256 devices in a mesh: grp: 32 (over x_lo, z, core), mem: 8 (over x_hi, y).
Axes of the slice: x: 4 (x_hi: 2, x_lo: 2; x = x_hi * 2 + x_lo), y: 4, z: 8, core: 2. Of those that a mesh axis runs over, the one named last changes fastest.
Arguments:
- queries: bfloat16 [16384, 32, 128], P('grp', 'mem'), may hold values from -16 to 16
- suffix_kv: bfloat16 [16384, 2, 4, 128], P('grp'), may hold values from -8 to 8
- prefix_kv: bfloat16 [256, 2, 128, 4, 128], P('grp'), may hold values from -8 to 8
- out_weight: bfloat16 [4096, 2048], P('mem'), may hold values from -0.09375 to 0.09375
- node_blocks: int32 [84], replicated, may hold values from 1 to 32, 256 in all
- root_of: int32 [16], replicated, may hold values from 0 to 3
- mid_of: int32 [64], replicated, may hold values from 0 to 15
Outputs:
- mixed: bfloat16 [16384, 2048], P(('grp', 'mem'))
The draws below stay inside these ranges and needn't reach their ends.
Inputs may be any that keep to these rules, and one draw needn't show every extreme that they name: `node_blocks`: some node has exactly 32 blocks, and all together have 256.
All inputs are finite; a program needn't handle non-finite values.
Results may differ from the reference program's by a relative error of at most 0.025.
Values may be sent and summed in bfloat16 or wider, within the bound.
A program may use at most 128 MiB of HBM per device.

```python
import math
import jax
import jax.numpy as jnp
import numpy as np
from jax import lax

D = 2048
QH = 32
KVH = 4
HD = 128
SUFFIX = 256
BLOCK = 128
MOST_BLK = 32
NBLK = 256
REQUESTS = 64
N0 = 4
N1 = 16
NODES = 84
TOKENS = 16384


def draw_queries(key, part):
    base_key = jax.random.fold_in(key, 11)
    sampled = jnp.clip(1.6 * jax.random.normal(base_key, (TOKENS, QH, HD), jnp.float32), -8.0, 8.0)
    return sampled.astype(jnp.bfloat16)


def draw_suffix_kv(key, part):
    base_key = jax.random.fold_in(key, 23)
    sampled = jnp.clip(1.6 * jax.random.normal(base_key, (TOKENS, 2, KVH, HD), jnp.float32), -8.0, 8.0)
    return sampled.astype(jnp.bfloat16)


def plant(entries, rng, smallest, top_value):
    index_at = [jax.random.randint(jax.random.fold_in(rng, axis), (), 0, length) for axis, length in enumerate(entries.shape)]
    main_axis = entries.shape.index(max(entries.shape))
    beside = index_at[:main_axis] + [(index_at[main_axis] + 1) % entries.shape[main_axis]] + index_at[main_axis + 1:]
    return entries.at[tuple(index_at)].set(smallest).at[tuple(beside)].set(top_value)


def levels(own_key, dims, pieces, least, high):
    factor_of, own = 1.0, jax.random.fold_in(own_key, 6)
    for dim, shards_of in pieces:
        steps = jnp.exp(jax.random.uniform(jax.random.fold_in(own, dim), (shards_of,), jnp.float32, least / len(pieces), high / len(pieces)))
        factor_of = factor_of * jnp.repeat(steps, dims[dim] // shards_of).reshape([-1 if axis == dim else 1 for axis in range(len(dims))])
    return factor_of


def profile(number_of, total, bound, slope):
    loads = [(1 << 20) // math.isqrt(grade ** slope) + 1 for grade in range(2, number_of + 1)]
    rest, holding = total - bound - (number_of - 1), [1] * (number_of - 1)
    while rest > 0:
        movable = [i for i in range(number_of - 1) if holding[i] < bound]
        whole, budget = sum([loads[i] for i in movable]), rest
        for i in movable:
            addition = min(bound - holding[i], max(1, budget * loads[i] // whole), rest)
            holding[i] = holding[i] + addition
            rest = rest - addition
    return np.array([bound] + holding)


def ragged(own_key, amount, total, bound, lean):
    if amount == 2:
        one = jax.random.randint(own_key, (), max(1, total - bound), min(bound, total - 1) + 1)
        return jnp.stack([one, total - one])
    lengths = jnp.asarray(profile(amount, total, bound, lean), jnp.int32)
    pairs = (amount - 1) // 2
    giver, taker = lengths[1:1 + 2 * pairs:2], lengths[2:2 + 2 * pairs:2]
    slack = jnp.minimum(giver - 1, bound - taker)
    moved = jax.random.randint(jax.random.fold_in(own_key, 1), (pairs,), 0, 1 << 20) % (slack + 1)
    lengths = lengths.at[1:1 + 2 * pairs:2].set(giver - moved).at[2:2 + 2 * pairs:2].set(taker + moved)
    return lengths[jax.random.permutation(jax.random.fold_in(own_key, 2), amount)]


def noise(own_key, extent, scale, limit, shards=(), kind=jnp.bfloat16):
    entries = scale * jax.random.normal(own_key, extent, jnp.float32)
    if shards:
        entries = entries * levels(own_key, extent, shards, -0.22, 0.18)
    return jnp.clip(entries, -limit, limit).astype(kind)


def setup_inputs(seed: int = 0) -> dict:
    arg_keys = jax.random.split(jax.random.key(seed), 8)
    queries = draw_queries(jax.random.fold_in(arg_keys[7], 71), 0)
    suffix_kv = draw_suffix_kv(jax.random.fold_in(arg_keys[7], 71), 0)
    prefix_kv = noise(arg_keys[2], (NBLK, 2, BLOCK, KVH, HD), 1.6, 8.0, ((0, 32),))
    out_weight = noise(arg_keys[3], (QH * HD, D), (QH * HD) ** -0.5, 0.09375, ((0, 8),))
    node_blocks = ragged(arg_keys[4], NODES, NBLK, MOST_BLK, 2).astype(jnp.int32)
    root_of = plant(jax.random.randint(arg_keys[5], (N1,), 0, N0), jax.random.fold_in(arg_keys[5], 1), 0, N0 - 1).astype(jnp.int32)
    mid_of = plant(jax.random.randint(arg_keys[6], (REQUESTS,), 0, N1), jax.random.fold_in(arg_keys[6], 1), 0, N1 - 1).astype(jnp.int32)
    return dict(queries=queries, suffix_kv=suffix_kv, prefix_kv=prefix_kv, out_weight=out_weight, node_blocks=node_blocks, root_of=root_of, mid_of=mid_of)


NEG = -1.0e30


def reference(queries, suffix_kv, prefix_kv, out_weight, node_blocks, root_of, mid_of):
    firsts = (jnp.cumsum(node_blocks) - node_blocks).astype(jnp.int32)
    slot_ids = jnp.arange(MOST_BLK, dtype=jnp.int32)
    causal = jnp.arange(SUFFIX)[:, None] >= jnp.arange(SUFFIX)[None, :]
    group_size = QH // KVH

    def one_request(request):
        middle = lax.dynamic_index_in_dim(mid_of, request, 0, keepdims=False)
        root_node = lax.dynamic_index_in_dim(root_of, middle, 0, keepdims=False)
        path_nodes = jnp.stack([root_node, N0 + middle, N0 + N1 + request]).astype(jnp.int32)
        starts = firsts[path_nodes]
        counts = node_blocks[path_nodes]
        in_node = slot_ids[None, :] < counts[:, None]
        block_ids = jnp.where(in_node, starts[:, None] + slot_ids[None, :], 0).reshape(-1).astype(jnp.int32)
        blocks = prefix_kv[block_ids]
        key_ok = jnp.repeat(in_node.reshape(-1), BLOCK)
        own_kv = lax.dynamic_slice_in_dim(suffix_kv, request * SUFFIX, SUFFIX, 0)
        own_q = lax.dynamic_slice_in_dim(queries, request * SUFFIX, SUFFIX, 0)
        allowed = jnp.concatenate([jnp.broadcast_to(key_ok[None, :], (SUFFIX, key_ok.shape[0])), causal], axis=1)
        heads_out = []
        for g in range(KVH):
            key_rows = jnp.concatenate([blocks[:, 0, :, g, :].reshape(-1, HD), own_kv[:, 0, g, :]], axis=0).astype(jnp.float32)
            value_rows = jnp.concatenate([blocks[:, 1, :, g, :].reshape(-1, HD), own_kv[:, 1, g, :]], axis=0).astype(jnp.float32)
            query_rows = own_q[:, g * group_size:(g + 1) * group_size, :].astype(jnp.float32)
            scores = jnp.einsum("sph,th->pst", query_rows, key_rows) * (HD ** -0.5)
            scores = jnp.where(allowed[None], scores, NEG)
            weights = jnp.exp(scores - jnp.max(scores, axis=-1, keepdims=True))
            totals = jnp.sum(weights, axis=-1)
            rounded = lax.optimization_barrier(weights.astype(jnp.bfloat16)).astype(jnp.float32)
            summed = jnp.einsum("pst,th->sph", rounded, value_rows)
            heads_out.append(summed / jnp.transpose(totals)[:, :, None])
        attended = jnp.concatenate(heads_out, axis=1).astype(jnp.bfloat16)
        return attended.reshape(SUFFIX, QH * HD)

    attention = lax.map(one_request, jnp.arange(REQUESTS, dtype=jnp.int32)).reshape(TOKENS, QH * HD)
    return jnp.dot(attention, out_weight, preferred_element_type=jnp.float32).astype(jnp.bfloat16)
```

```python
import functools

import jax
import jax.numpy as jnp
from jax import lax
from jax.experimental import pallas as pl
from jax.experimental.pallas import tpu as pltpu
from jax.sharding import PartitionSpec as P

QH = 32
KVH = 4
SUFFIX = 256
MOST_BLK = 32
NEG = -1e30
MESH = pl.DeviceIdType.MESH


def path_table(request_ids, node_blocks, root_of, mid_of):
    nodes_all = node_blocks.shape[0]
    middles_all = root_of.shape[0]
    leaves = mid_of.shape[0]
    roots_all = nodes_all - middles_all - leaves
    firsts = jnp.cumsum(node_blocks) - node_blocks
    middles = jnp.sum(
        jnp.where(jnp.arange(leaves)[None, :] == request_ids[:, None], mid_of[None, :], 0), axis=1
    )
    root_ids = jnp.sum(
        jnp.where(jnp.arange(middles_all)[None, :] == middles[:, None], root_of[None, :], 0), axis=1
    )
    path_nodes = jnp.stack(
        [root_ids, roots_all + middles, roots_all + middles_all + request_ids], axis=1
    )
    picked = jnp.arange(nodes_all)[None, None, :] == path_nodes[:, :, None]
    starts = jnp.sum(jnp.where(picked, firsts[None, None, :], 0), axis=2)
    counts = jnp.sum(jnp.where(picked, node_blocks[None, None, :], 0), axis=2)
    ends = jnp.cumsum(counts, axis=1)
    begins = ends - counts
    slots = jnp.arange(3 * MOST_BLK)[None, :]
    which = (slots >= ends[:, 0:1]).astype(jnp.int32) + (slots >= ends[:, 1:2]).astype(jnp.int32)
    which = jnp.minimum(which, 2)
    pick = jnp.arange(3)[None, None, :] == which[:, :, None]
    start_of = jnp.sum(jnp.where(pick, starts[:, None, :], 0), axis=2)
    begin_of = jnp.sum(jnp.where(pick, begins[:, None, :], 0), axis=2)
    ids = start_of + slots - begin_of
    total = ends[:, 2]
    ids = jnp.where(slots < total[:, None], ids, 0)
    return ids.astype(jnp.int32), total.astype(jnp.int32)


def attend_kernel(slots, ids_ref, cnt_ref, q_ref, ks_ref, vs_ref, kv_hbm, o_ref, buf, sem, m_sc, l_sc, acc_sc):
    j = pl.program_id(0)
    n = cnt_ref[j]
    rows, hd = q_ref.shape
    scale = hd ** (-0.5)
    contract = (((1,), (1,)), ((), ()))
    q = q_ref[...]

    scores = lax.dot_general(q, ks_ref[...], contract, preferred_element_type=jnp.float32) * scale
    tok = lax.broadcasted_iota(jnp.int32, scores.shape, 0) % SUFFIX
    key = lax.broadcasted_iota(jnp.int32, scores.shape, 1)
    scores = jnp.where(key <= tok, scores, NEG)
    high = jnp.max(scores, axis=-1, keepdims=True)
    weights = jnp.exp(scores - high)
    m_sc[...] = high
    l_sc[...] = jnp.sum(weights, axis=-1, keepdims=True)
    acc_sc[...] = jnp.dot(weights.astype(jnp.bfloat16), vs_ref[...], preferred_element_type=jnp.float32)

    def fetch(i, slot):
        pltpu.make_async_copy(kv_hbm.at[ids_ref[j * slots + i]], buf.at[slot], sem.at[slot]).start()

    @pl.when(n > 0)
    def _():
        fetch(0, 0)

    def body(i, carry):
        slot = i % 2
        pltpu.make_async_copy(kv_hbm.at[0], buf.at[slot], sem.at[slot]).wait()

        @pl.when(i + 1 < n)
        def _():
            fetch(i + 1, 1 - slot)

        s = lax.dot_general(q, buf[slot, 0], contract, preferred_element_type=jnp.float32) * scale
        m_old = m_sc[...]
        m_new = jnp.maximum(m_old, jnp.max(s, axis=-1, keepdims=True))
        factor = jnp.exp(m_old - m_new)
        p = jnp.exp(s - m_new)
        l_sc[...] = l_sc[...] * factor + jnp.sum(p, axis=-1, keepdims=True)
        acc_sc[...] = acc_sc[...] * factor + jnp.dot(
            p.astype(jnp.bfloat16), buf[slot, 1], preferred_element_type=jnp.float32
        )
        m_sc[...] = m_new
        return carry

    lax.fori_loop(0, n, body, 0)
    o_ref[...] = (acc_sc[...] / l_sc[...]).astype(o_ref.dtype)


def attend(ids, counts, q, ks, vs, kv_all):
    req, rows, hd = q.shape
    slots = ids.shape[1]
    block_shape = kv_all.shape[1:]
    return pl.pallas_call(
        functools.partial(attend_kernel, slots),
        out_shape=jax.ShapeDtypeStruct((req, rows, hd), jnp.bfloat16),
        grid_spec=pltpu.PrefetchScalarGridSpec(
            num_scalar_prefetch=2,
            grid=(req,),
            in_specs=[
                pl.BlockSpec((None, rows, hd), lambda j, ids, cnt: (j, 0, 0)),
                pl.BlockSpec((None, SUFFIX, hd), lambda j, ids, cnt: (j, 0, 0)),
                pl.BlockSpec((None, SUFFIX, hd), lambda j, ids, cnt: (j, 0, 0)),
                pl.BlockSpec(memory_space=pl.ANY),
            ],
            out_specs=pl.BlockSpec((None, rows, hd), lambda j, ids, cnt: (j, 0, 0)),
            scratch_shapes=[
                pltpu.VMEM((2,) + block_shape, kv_all.dtype),
                pltpu.SemaphoreType.DMA((2,)),
                pltpu.VMEM((rows, 1), jnp.float32),
                pltpu.VMEM((rows, 1), jnp.float32),
                pltpu.VMEM((rows, hd), jnp.float32),
            ],
        ),
        compiler_params=pltpu.CompilerParams(dimension_semantics=("arbitrary",)),
    )(ids.reshape(-1), counts, q, ks, vs, kv_all)


def exchange_kernel(n, x_ref, o_ref, recv, send_sem, recv_sem):
    me = lax.axis_index("mem")
    grp = lax.axis_index("grp")
    barrier = pltpu.get_barrier_semaphore()
    for k in range(1, n):
        pl.semaphore_signal(barrier, inc=1, device_id=(grp, lax.rem(me + k, n)), device_id_type=MESH)
    pl.semaphore_wait(barrier, n - 1)
    copies = []
    for k in range(1, n):
        peer = lax.rem(me + k, n)
        copy = pltpu.make_async_remote_copy(
            src_ref=x_ref.at[peer],
            dst_ref=recv.at[k],
            send_sem=send_sem.at[k],
            recv_sem=recv_sem.at[k],
            device_id=(grp, peer),
            device_id_type=MESH,
        )
        copy.start()
        copies.append(copy)
    total = x_ref[me].astype(jnp.float32)
    for k in range(1, n):
        copies[k - 1].wait()
        total = total + recv[k].astype(jnp.float32)
    o_ref[...] = total.astype(o_ref.dtype)


def exchange_sum(x):
    n, rows, cols = x.shape
    return pl.pallas_call(
        functools.partial(exchange_kernel, n),
        out_shape=jax.ShapeDtypeStruct((rows, cols), x.dtype),
        in_specs=[pl.BlockSpec(memory_space=pltpu.VMEM)],
        out_specs=pl.BlockSpec(memory_space=pltpu.VMEM),
        scratch_shapes=[
            pltpu.VMEM((n, rows, cols), x.dtype),
            pltpu.SemaphoreType.DMA((n,)),
            pltpu.SemaphoreType.DMA((n,)),
        ],
        compiler_params=pltpu.CompilerParams(collective_id=0, has_side_effects=True),
    )(x)


def on_device(n_mem, queries, suffix_kv, prefix_kv, out_weight, node_blocks, root_of, mid_of):
    group_index = lax.axis_index("grp")
    head_index = lax.axis_index("mem")
    tokens_dev, heads_dev, head_dim = queries.shape
    req_local = tokens_dev // SUFFIX
    group_size = QH // KVH
    kv_start = head_index * heads_dev // group_size
    prefix_part = lax.dynamic_index_in_dim(prefix_kv, kv_start, 3, keepdims=False)
    suffix_part = lax.dynamic_index_in_dim(suffix_kv, kv_start, 2, keepdims=False)
    kv_all = lax.all_gather(prefix_part, "grp", axis=0, tiled=True)

    request_ids = group_index * req_local + jnp.arange(req_local)
    ids, counts = path_table(request_ids, node_blocks, root_of, mid_of)

    q = queries.reshape(req_local, SUFFIX, heads_dev, head_dim).transpose(0, 2, 1, 3)
    q = q.reshape(req_local, heads_dev * SUFFIX, head_dim)
    ks = suffix_part[:, 0].reshape(req_local, SUFFIX, head_dim)
    vs = suffix_part[:, 1].reshape(req_local, SUFFIX, head_dim)
    attended = attend(ids, counts, q, ks, vs, kv_all)
    attended = attended.reshape(req_local, heads_dev, SUFFIX, head_dim)
    w = out_weight.reshape(heads_dev, head_dim, out_weight.shape[1])
    partial = lax.dot_general(
        attended, w, (((1, 3), (0, 1)), ((), ())), preferred_element_type=jnp.float32
    ).astype(jnp.bfloat16)
    partial = partial.reshape(tokens_dev, out_weight.shape[1])
    partial = partial.reshape(n_mem, tokens_dev // n_mem, out_weight.shape[1])
    return exchange_sum(partial)


def solution(mesh):
    return jax.shard_map(
        functools.partial(on_device, mesh.shape["mem"]),
        mesh=mesh,
        in_specs=(
            P("grp", "mem", None),
            P("grp", None, None, None),
            P("grp", None, None, None, None),
            P("mem", None),
            P(),
            P(),
            P(),
        ),
        out_specs=P(("grp", "mem"), None),
        check_vma=False,
    )
```

```python
import functools

import jax
import jax.numpy as jnp
from jax import lax
from jax.experimental import pallas as pl
from jax.experimental.pallas import tpu as pltpu
from jax.sharding import Mesh, PartitionSpec as P

QH = 32
KVH = 4
SUFFIX = 256
MOST_BLK = 32
NEG = -1e30
MESH = pl.DeviceIdType.MESH


def path_table(request_ids, node_blocks, root_of, mid_of):
    nodes_all = node_blocks.shape[0]
    middles_all = root_of.shape[0]
    leaves = mid_of.shape[0]
    roots_all = nodes_all - middles_all - leaves
    firsts = jnp.cumsum(node_blocks) - node_blocks
    middles = jnp.sum(
        jnp.where(jnp.arange(leaves)[None, :] == request_ids[:, None], mid_of[None, :], 0), axis=1
    )
    root_ids = jnp.sum(
        jnp.where(jnp.arange(middles_all)[None, :] == middles[:, None], root_of[None, :], 0), axis=1
    )
    path_nodes = jnp.stack(
        [root_ids, roots_all + middles, roots_all + middles_all + request_ids], axis=1
    )
    picked = jnp.arange(nodes_all)[None, None, :] == path_nodes[:, :, None]
    starts = jnp.sum(jnp.where(picked, firsts[None, None, :], 0), axis=2)
    counts = jnp.sum(jnp.where(picked, node_blocks[None, None, :], 0), axis=2)
    ends = jnp.cumsum(counts, axis=1)
    begins = ends - counts
    slots = jnp.arange(3 * MOST_BLK)[None, :]
    which = (slots >= ends[:, 0:1]).astype(jnp.int32) + (slots >= ends[:, 1:2]).astype(jnp.int32)
    which = jnp.minimum(which, 2)
    pick = jnp.arange(3)[None, None, :] == which[:, :, None]
    start_of = jnp.sum(jnp.where(pick, starts[:, None, :], 0), axis=2)
    begin_of = jnp.sum(jnp.where(pick, begins[:, None, :], 0), axis=2)
    ids = start_of + slots - begin_of
    total = ends[:, 2]
    ids = jnp.where(slots < total[:, None], ids, 0)
    return ids.astype(jnp.int32), total.astype(jnp.int32)


def attend_kernel(slots, ids_ref, cnt_ref, q_ref, ks_ref, vs_ref, kv_hbm, o_ref, buf, sem, m_sc, l_sc, acc_sc):
    j = pl.program_id(0)
    n = cnt_ref[j]
    rows, hd = q_ref.shape
    scale = hd ** (-0.5)
    contract = (((1,), (1,)), ((), ()))
    q = q_ref[...]

    scores = lax.dot_general(q, ks_ref[...], contract, preferred_element_type=jnp.float32) * scale
    tok = lax.broadcasted_iota(jnp.int32, scores.shape, 0) % SUFFIX
    key = lax.broadcasted_iota(jnp.int32, scores.shape, 1)
    scores = jnp.where(key <= tok, scores, NEG)
    high = jnp.max(scores, axis=-1, keepdims=True)
    weights = jnp.exp(scores - high)
    m_sc[...] = high
    l_sc[...] = jnp.sum(weights, axis=-1, keepdims=True)
    acc_sc[...] = jnp.dot(weights.astype(jnp.bfloat16), vs_ref[...], preferred_element_type=jnp.float32)

    def fetch(i, slot):
        pltpu.make_async_copy(kv_hbm.at[ids_ref[j * slots + i]], buf.at[slot], sem.at[slot]).start()

    @pl.when(n > 0)
    def _():
        fetch(0, 0)

    def body(i, carry):
        slot = i % 2
        pltpu.make_async_copy(kv_hbm.at[0], buf.at[slot], sem.at[slot]).wait()

        @pl.when(i + 1 < n)
        def _():
            fetch(i + 1, 1 - slot)

        s = lax.dot_general(q, buf[slot, 0], contract, preferred_element_type=jnp.float32) * scale
        m_old = m_sc[...]
        m_new = jnp.maximum(m_old, jnp.max(s, axis=-1, keepdims=True))
        factor = jnp.exp(m_old - m_new)
        p = jnp.exp(s - m_new)
        l_sc[...] = l_sc[...] * factor + jnp.sum(p, axis=-1, keepdims=True)
        acc_sc[...] = acc_sc[...] * factor + jnp.dot(
            p.astype(jnp.bfloat16), buf[slot, 1], preferred_element_type=jnp.float32
        )
        m_sc[...] = m_new
        return carry

    lax.fori_loop(0, n, body, 0)
    o_ref[...] = (acc_sc[...] / l_sc[...]).astype(o_ref.dtype)


def attend(ids, counts, q, ks, vs, kv_all):
    req, rows, hd = q.shape
    slots = ids.shape[1]
    block_shape = kv_all.shape[1:]
    return pl.pallas_call(
        functools.partial(attend_kernel, slots),
        out_shape=jax.ShapeDtypeStruct((req, rows, hd), jnp.bfloat16),
        grid_spec=pltpu.PrefetchScalarGridSpec(
            num_scalar_prefetch=2,
            grid=(req,),
            in_specs=[
                pl.BlockSpec((None, rows, hd), lambda j, ids, cnt: (j, 0, 0)),
                pl.BlockSpec((None, SUFFIX, hd), lambda j, ids, cnt: (j, 0, 0)),
                pl.BlockSpec((None, SUFFIX, hd), lambda j, ids, cnt: (j, 0, 0)),
                pl.BlockSpec(memory_space=pl.ANY),
            ],
            out_specs=pl.BlockSpec((None, rows, hd), lambda j, ids, cnt: (j, 0, 0)),
            scratch_shapes=[
                pltpu.VMEM((2,) + block_shape, kv_all.dtype),
                pltpu.SemaphoreType.DMA((2,)),
                pltpu.VMEM((rows, 1), jnp.float32),
                pltpu.VMEM((rows, 1), jnp.float32),
                pltpu.VMEM((rows, hd), jnp.float32),
            ],
        ),
        compiler_params=pltpu.CompilerParams(dimension_semantics=("arbitrary",)),
    )(ids.reshape(-1), counts, q, ks, vs, kv_all)


def exchange_kernel(n, x_ref, o_ref, recv, send_sem, recv_sem):
    me = lax.axis_index("mem")
    grp = (lax.axis_index("chip"), lax.axis_index("core"))
    barrier = pltpu.get_barrier_semaphore()
    for k in range(1, n):
        pl.semaphore_signal(barrier, inc=1, device_id=grp + (lax.rem(me + k, n),), device_id_type=MESH)
    pl.semaphore_wait(barrier, n - 1)
    copies = []
    for k in range(1, n):
        peer = lax.rem(me + k, n)
        copy = pltpu.make_async_remote_copy(
            src_ref=x_ref.at[peer],
            dst_ref=recv.at[k],
            send_sem=send_sem.at[k],
            recv_sem=recv_sem.at[k],
            device_id=grp + (peer,),
            device_id_type=MESH,
        )
        copy.start()
        copies.append(copy)
    total = x_ref[me].astype(jnp.float32)
    for k in range(1, n):
        copies[k - 1].wait()
        total = total + recv[k].astype(jnp.float32)
    o_ref[...] = total.astype(o_ref.dtype)


def exchange_sum(x):
    n, rows, cols = x.shape
    return pl.pallas_call(
        functools.partial(exchange_kernel, n),
        out_shape=jax.ShapeDtypeStruct((rows, cols), x.dtype),
        in_specs=[pl.BlockSpec(memory_space=pltpu.VMEM)],
        out_specs=pl.BlockSpec(memory_space=pltpu.VMEM),
        scratch_shapes=[
            pltpu.VMEM((n, rows, cols), x.dtype),
            pltpu.SemaphoreType.DMA((n,)),
            pltpu.SemaphoreType.DMA((n,)),
        ],
        compiler_params=pltpu.CompilerParams(collective_id=0, has_side_effects=True),
    )(x)


def on_device(n_mem, n_core, queries, suffix_kv, prefix_kv, out_weight, node_blocks, root_of, mid_of):
    group_index = lax.axis_index("chip") * n_core + lax.axis_index("core")
    head_index = lax.axis_index("mem")
    tokens_dev, heads_dev, head_dim = queries.shape
    req_local = tokens_dev // SUFFIX
    group_size = QH // KVH
    kv_start = head_index * heads_dev // group_size
    prefix_part = lax.dynamic_index_in_dim(prefix_kv, kv_start, 3, keepdims=False)
    suffix_part = lax.dynamic_index_in_dim(suffix_kv, kv_start, 2, keepdims=False)
    own_blocks = prefix_part.shape[0]
    kv_half = lax.all_gather(prefix_part, "chip", axis=0, tiled=True)
    kv_all = lax.all_gather(kv_half, "core", axis=0, tiled=True)

    request_ids = group_index * req_local + jnp.arange(req_local)
    ids, counts = path_table(request_ids, node_blocks, root_of, mid_of)
    owner = ids // own_blocks
    ids = (owner % n_core) * kv_half.shape[0] + (owner // n_core) * own_blocks + ids % own_blocks

    q = queries.reshape(req_local, SUFFIX, heads_dev, head_dim).transpose(0, 2, 1, 3)
    q = q.reshape(req_local, heads_dev * SUFFIX, head_dim)
    ks = suffix_part[:, 0].reshape(req_local, SUFFIX, head_dim)
    vs = suffix_part[:, 1].reshape(req_local, SUFFIX, head_dim)
    attended = attend(ids, counts, q, ks, vs, kv_all)
    attended = attended.reshape(req_local, heads_dev, SUFFIX, head_dim)
    w = out_weight.reshape(heads_dev, head_dim, out_weight.shape[1])
    partial = lax.dot_general(
        attended, w, (((1, 3), (0, 1)), ((), ())), preferred_element_type=jnp.float32
    ).astype(jnp.bfloat16)
    partial = partial.reshape(tokens_dev, out_weight.shape[1])
    partial = partial.reshape(n_mem, tokens_dev // n_mem, out_weight.shape[1])
    return exchange_sum(partial)


def solution(mesh):
    n_core = 2
    n_grp, n_mem = mesh.shape["grp"], mesh.shape["mem"]
    fine = Mesh(mesh.devices.reshape(n_grp // n_core, n_core, n_mem), ("chip", "core", "mem"))
    grp = ("chip", "core")
    return jax.shard_map(
        functools.partial(on_device, n_mem, n_core),
        mesh=fine,
        in_specs=(
            P(grp, "mem", None),
            P(grp, None, None, None),
            P(grp, None, None, None, None),
            P("mem", None),
            P(),
            P(),
            P(),
        ),
        out_specs=P(grp + ("mem",), None),
        check_vma=False,
    )
```

```python
import functools

import jax
import jax.numpy as jnp
from jax import lax
from jax.experimental import pallas as pl
from jax.experimental.pallas import tpu as pltpu
from jax.sharding import PartitionSpec as P

QH = 32
KVH = 4
SUFFIX = 256
MOST_BLK = 32
N_CHUNK = 4
NEG = -1e30
MESH = pl.DeviceIdType.MESH


def path_table(request_ids, node_blocks, root_of, mid_of):
    nodes_all = node_blocks.shape[0]
    middles_all = root_of.shape[0]
    leaves = mid_of.shape[0]
    roots_all = nodes_all - middles_all - leaves
    firsts = jnp.cumsum(node_blocks) - node_blocks
    middles = jnp.sum(
        jnp.where(jnp.arange(leaves)[None, :] == request_ids[:, None], mid_of[None, :], 0), axis=1
    )
    root_ids = jnp.sum(
        jnp.where(jnp.arange(middles_all)[None, :] == middles[:, None], root_of[None, :], 0), axis=1
    )
    path_nodes = jnp.stack(
        [root_ids, roots_all + middles, roots_all + middles_all + request_ids], axis=1
    )
    picked = jnp.arange(nodes_all)[None, None, :] == path_nodes[:, :, None]
    starts = jnp.sum(jnp.where(picked, firsts[None, None, :], 0), axis=2)
    counts = jnp.sum(jnp.where(picked, node_blocks[None, None, :], 0), axis=2)
    ends = jnp.cumsum(counts, axis=1)
    begins = ends - counts
    slots = jnp.arange(3 * MOST_BLK)[None, :]
    which = (slots >= ends[:, 0:1]).astype(jnp.int32) + (slots >= ends[:, 1:2]).astype(jnp.int32)
    which = jnp.minimum(which, 2)
    pick = jnp.arange(3)[None, None, :] == which[:, :, None]
    start_of = jnp.sum(jnp.where(pick, starts[:, None, :], 0), axis=2)
    begin_of = jnp.sum(jnp.where(pick, begins[:, None, :], 0), axis=2)
    ids = start_of + slots - begin_of
    total = ends[:, 2]
    ids = jnp.where(slots < total[:, None], ids, 0)
    return ids.astype(jnp.int32), total.astype(jnp.int32)


def suffix_kernel(q_ref, ks_ref, vs_ref, m_ref, l_ref, acc_ref):
    hd = q_ref.shape[-1]
    contract = (((1,), (1,)), ((), ()))
    scores = lax.dot_general(q_ref[...], ks_ref[...], contract, preferred_element_type=jnp.float32)
    scores = scores * hd ** (-0.5)
    tok = lax.broadcasted_iota(jnp.int32, scores.shape, 0) % SUFFIX
    key = lax.broadcasted_iota(jnp.int32, scores.shape, 1)
    scores = jnp.where(key <= tok, scores, NEG)
    high = jnp.max(scores, axis=-1, keepdims=True)
    weights = jnp.exp(scores - high)
    m_ref[...] = high
    l_ref[...] = jnp.sum(weights, axis=-1, keepdims=True)
    acc_ref[...] = jnp.dot(weights.astype(jnp.bfloat16), vs_ref[...], preferred_element_type=jnp.float32)


def state_shapes(req, rows, hd):
    return (
        jax.ShapeDtypeStruct((req, rows, 1), jnp.float32),
        jax.ShapeDtypeStruct((req, rows, 1), jnp.float32),
        jax.ShapeDtypeStruct((req, rows, hd), jnp.float32),
    )


def state_specs(rows, hd, index):
    return [
        pl.BlockSpec((None, rows, 1), index),
        pl.BlockSpec((None, rows, 1), index),
        pl.BlockSpec((None, rows, hd), index),
    ]


def suffix_part_attend(q, ks, vs):
    req, rows, hd = q.shape
    index = lambda j: (j, 0, 0)
    return pl.pallas_call(
        suffix_kernel,
        out_shape=state_shapes(req, rows, hd),
        grid=(req,),
        in_specs=[
            pl.BlockSpec((None, rows, hd), index),
            pl.BlockSpec((None, SUFFIX, hd), index),
            pl.BlockSpec((None, SUFFIX, hd), index),
        ],
        out_specs=state_specs(rows, hd, index),
        compiler_params=pltpu.CompilerParams(dimension_semantics=("arbitrary",)),
    )(q, ks, vs)


def chunk_kernel(slots, ids_ref, off_ref, cnt_ref, q_ref, kv_hbm, m_ref, l_ref, acc_ref, buf, sem):
    j = pl.program_id(0)
    n = cnt_ref[j]
    base = j * slots + off_ref[j]
    hd = q_ref.shape[-1]
    scale = hd ** (-0.5)
    contract = (((1,), (1,)), ((), ()))
    q = q_ref[...]
    m_ref[...] = jnp.full(m_ref.shape, NEG, jnp.float32)
    l_ref[...] = jnp.zeros(l_ref.shape, jnp.float32)
    acc_ref[...] = jnp.zeros(acc_ref.shape, jnp.float32)

    def fetch(i, slot):
        pltpu.make_async_copy(kv_hbm.at[ids_ref[base + i]], buf.at[slot], sem.at[slot]).start()

    @pl.when(n > 0)
    def _():
        fetch(0, 0)

    def body(i, carry):
        slot = i % 2
        pltpu.make_async_copy(kv_hbm.at[0], buf.at[slot], sem.at[slot]).wait()

        @pl.when(i + 1 < n)
        def _():
            fetch(i + 1, 1 - slot)

        s = lax.dot_general(q, buf[slot, 0], contract, preferred_element_type=jnp.float32) * scale
        m_old = m_ref[...]
        m_new = jnp.maximum(m_old, jnp.max(s, axis=-1, keepdims=True))
        factor = jnp.exp(m_old - m_new)
        p = jnp.exp(s - m_new)
        l_ref[...] = l_ref[...] * factor + jnp.sum(p, axis=-1, keepdims=True)
        acc_ref[...] = acc_ref[...] * factor + jnp.dot(
            p.astype(jnp.bfloat16), buf[slot, 1], preferred_element_type=jnp.float32
        )
        m_ref[...] = m_new
        return carry

    lax.fori_loop(0, n, body, 0)


def chunk_attend(ids, offs, cnts, q, kv_chunk):
    req, rows, hd = q.shape
    slots = ids.shape[1]
    block_shape = kv_chunk.shape[1:]
    index = lambda j, ids, off, cnt: (j, 0, 0)
    return pl.pallas_call(
        functools.partial(chunk_kernel, slots),
        out_shape=state_shapes(req, rows, hd),
        grid_spec=pltpu.PrefetchScalarGridSpec(
            num_scalar_prefetch=3,
            grid=(req,),
            in_specs=[
                pl.BlockSpec((None, rows, hd), index),
                pl.BlockSpec(memory_space=pl.ANY),
            ],
            out_specs=state_specs(rows, hd, index),
            scratch_shapes=[
                pltpu.VMEM((2,) + block_shape, kv_chunk.dtype),
                pltpu.SemaphoreType.DMA((2,)),
            ],
        ),
        compiler_params=pltpu.CompilerParams(dimension_semantics=("arbitrary",)),
    )(ids.reshape(-1), offs, cnts, q, kv_chunk)


def exchange_kernel(n, x_ref, o_ref, recv, send_sem, recv_sem):
    me = lax.axis_index("mem")
    grp = lax.axis_index("grp")
    barrier = pltpu.get_barrier_semaphore()
    for k in range(1, n):
        pl.semaphore_signal(barrier, inc=1, device_id=(grp, lax.rem(me + k, n)), device_id_type=MESH)
    pl.semaphore_wait(barrier, n - 1)
    copies = []
    for k in range(1, n):
        peer = lax.rem(me + k, n)
        copy = pltpu.make_async_remote_copy(
            src_ref=x_ref.at[peer],
            dst_ref=recv.at[k],
            send_sem=send_sem.at[k],
            recv_sem=recv_sem.at[k],
            device_id=(grp, peer),
            device_id_type=MESH,
        )
        copy.start()
        copies.append(copy)
    total = x_ref[me].astype(jnp.float32)
    for k in range(1, n):
        copies[k - 1].wait()
        total = total + recv[k].astype(jnp.float32)
    o_ref[...] = total.astype(o_ref.dtype)


def exchange_sum(x):
    n, rows, cols = x.shape
    return pl.pallas_call(
        functools.partial(exchange_kernel, n),
        out_shape=jax.ShapeDtypeStruct((rows, cols), x.dtype),
        in_specs=[pl.BlockSpec(memory_space=pltpu.VMEM)],
        out_specs=pl.BlockSpec(memory_space=pltpu.VMEM),
        scratch_shapes=[
            pltpu.VMEM((n, rows, cols), x.dtype),
            pltpu.SemaphoreType.DMA((n,)),
            pltpu.SemaphoreType.DMA((n,)),
        ],
        compiler_params=pltpu.CompilerParams(collective_id=0, has_side_effects=True),
    )(x)


def on_device(n_mem, queries, suffix_kv, prefix_kv, out_weight, node_blocks, root_of, mid_of):
    group_index = lax.axis_index("grp")
    head_index = lax.axis_index("mem")
    tokens_dev, heads_dev, head_dim = queries.shape
    req_local = tokens_dev // SUFFIX
    group_size = QH // KVH
    kv_start = head_index * heads_dev // group_size
    prefix_part = lax.dynamic_index_in_dim(prefix_kv, kv_start, 3, keepdims=False)
    suffix_part = lax.dynamic_index_in_dim(suffix_kv, kv_start, 2, keepdims=False)
    own_blocks = prefix_part.shape[0]
    per_chunk = own_blocks // N_CHUNK

    request_ids = group_index * req_local + jnp.arange(req_local)
    ids, counts = path_table(request_ids, node_blocks, root_of, mid_of)
    slots = jnp.arange(ids.shape[1])[None, :]
    valid = slots < counts[:, None]
    chunk_of = (ids % own_blocks) // per_chunk
    place = (ids // own_blocks) * per_chunk + ids % per_chunk
    order = jnp.argsort(jnp.where(valid, chunk_of, N_CHUNK) * ids.shape[1] + slots, axis=1)
    place = jnp.take_along_axis(place, order, axis=1).astype(jnp.int32)
    chunk_sorted = jnp.take_along_axis(jnp.where(valid, chunk_of, N_CHUNK), order, axis=1)
    cnts = jnp.sum(chunk_sorted[:, :, None] == jnp.arange(N_CHUNK)[None, None, :], axis=1).astype(jnp.int32)
    offs = (jnp.cumsum(cnts, axis=1) - cnts).astype(jnp.int32)

    q = queries.reshape(req_local, SUFFIX, heads_dev, head_dim).transpose(0, 2, 1, 3)
    q = q.reshape(req_local, heads_dev * SUFFIX, head_dim)
    ks = suffix_part[:, 0].reshape(req_local, SUFFIX, head_dim)
    vs = suffix_part[:, 1].reshape(req_local, SUFFIX, head_dim)
    parts = [suffix_part_attend(q, ks, vs)]
    for c in range(N_CHUNK):
        kv_chunk = lax.all_gather(
            prefix_part[c * per_chunk : (c + 1) * per_chunk], "grp", axis=0, tiled=True
        )
        parts.append(chunk_attend(place, offs[:, c], cnts[:, c], q, kv_chunk))
    high = parts[0][0]
    for m_c, _, _ in parts[1:]:
        high = jnp.maximum(high, m_c)
    total = 0.0
    summed = 0.0
    for m_c, l_c, acc_c in parts:
        factor = jnp.exp(m_c - high)
        total = total + l_c * factor
        summed = summed + acc_c * factor
    attended = (summed / total).astype(jnp.bfloat16)
    attended = attended.reshape(req_local, heads_dev, SUFFIX, head_dim)
    w = out_weight.reshape(heads_dev, head_dim, out_weight.shape[1])
    partial = lax.dot_general(
        attended, w, (((1, 3), (0, 1)), ((), ())), preferred_element_type=jnp.float32
    ).astype(jnp.bfloat16)
    partial = partial.reshape(tokens_dev, out_weight.shape[1])
    partial = partial.reshape(n_mem, tokens_dev // n_mem, out_weight.shape[1])
    return exchange_sum(partial)


def solution(mesh):
    return jax.shard_map(
        functools.partial(on_device, mesh.shape["mem"]),
        mesh=mesh,
        in_specs=(
            P("grp", "mem", None),
            P("grp", None, None, None),
            P("grp", None, None, None, None),
            P("mem", None),
            P(),
            P(),
            P(),
        ),
        out_specs=P(("grp", "mem"), None),
        check_vma=False,
    )
```

```python
import functools

import jax
import jax.numpy as jnp
from jax import lax
from jax.experimental import pallas as pl
from jax.experimental.pallas import tpu as pltpu
from jax.sharding import PartitionSpec as P

QH = 32
KVH = 4
SUFFIX = 256
MOST_BLK = 32
N_BUF = 4
NEG = -1e30
MESH = pl.DeviceIdType.MESH


def path_table(request_ids, node_blocks, root_of, mid_of):
    nodes_all = node_blocks.shape[0]
    middles_all = root_of.shape[0]
    leaves = mid_of.shape[0]
    roots_all = nodes_all - middles_all - leaves
    firsts = jnp.cumsum(node_blocks) - node_blocks
    middles = jnp.sum(
        jnp.where(jnp.arange(leaves)[None, :] == request_ids[:, None], mid_of[None, :], 0), axis=1
    )
    root_ids = jnp.sum(
        jnp.where(jnp.arange(middles_all)[None, :] == middles[:, None], root_of[None, :], 0), axis=1
    )
    path_nodes = jnp.stack(
        [root_ids, roots_all + middles, roots_all + middles_all + request_ids], axis=1
    )
    picked = jnp.arange(nodes_all)[None, None, :] == path_nodes[:, :, None]
    starts = jnp.sum(jnp.where(picked, firsts[None, None, :], 0), axis=2)
    counts = jnp.sum(jnp.where(picked, node_blocks[None, None, :], 0), axis=2)
    ends = jnp.cumsum(counts, axis=1)
    begins = ends - counts
    slots = jnp.arange(3 * MOST_BLK)[None, :]
    which = (slots >= ends[:, 0:1]).astype(jnp.int32) + (slots >= ends[:, 1:2]).astype(jnp.int32)
    which = jnp.minimum(which, 2)
    pick = jnp.arange(3)[None, None, :] == which[:, :, None]
    start_of = jnp.sum(jnp.where(pick, starts[:, None, :], 0), axis=2)
    begin_of = jnp.sum(jnp.where(pick, begins[:, None, :], 0), axis=2)
    ids = start_of + slots - begin_of
    total = ends[:, 2]
    ids = jnp.where(slots < total[:, None], ids, 0)
    return ids.astype(jnp.int32), total.astype(jnp.int32)


def attend_kernel(slots, ids_ref, cnt_ref, q_ref, ks_ref, vs_ref, kv_hbm, o_ref, buf, sem, m_sc, l_sc, acc_sc):
    j = pl.program_id(0)
    n = cnt_ref[j]
    rows, hd = q_ref.shape
    scale = hd ** (-0.5)
    contract = (((1,), (1,)), ((), ()))
    q = q_ref[...]

    scores = lax.dot_general(q, ks_ref[...], contract, preferred_element_type=jnp.float32) * scale
    tok = lax.broadcasted_iota(jnp.int32, scores.shape, 0) % SUFFIX
    key = lax.broadcasted_iota(jnp.int32, scores.shape, 1)
    scores = jnp.where(key <= tok, scores, NEG)
    high = jnp.max(scores, axis=-1, keepdims=True)
    weights = jnp.exp(scores - high)
    m_sc[...] = high
    l_sc[...] = jnp.sum(weights, axis=-1, keepdims=True)
    acc_sc[...] = jnp.dot(weights.astype(jnp.bfloat16), vs_ref[...], preferred_element_type=jnp.float32)

    def fetch(i, slot):
        pltpu.make_async_copy(kv_hbm.at[ids_ref[j * slots + i]], buf.at[slot], sem.at[slot]).start()

    ahead = N_BUF - 1
    for t in range(ahead):

        @pl.when(t < n)
        def _():
            fetch(t, t)

    def body(i, carry):
        slot = i % N_BUF
        pltpu.make_async_copy(kv_hbm.at[0], buf.at[slot], sem.at[slot]).wait()

        @pl.when(i + ahead < n)
        def _():
            fetch(i + ahead, (i + ahead) % N_BUF)

        s = lax.dot_general(q, buf[slot, 0], contract, preferred_element_type=jnp.float32) * scale
        m_old = m_sc[...]
        m_new = jnp.maximum(m_old, jnp.max(s, axis=-1, keepdims=True))
        factor = jnp.exp(m_old - m_new)
        p = jnp.exp(s - m_new)
        l_sc[...] = l_sc[...] * factor + jnp.sum(p, axis=-1, keepdims=True)
        acc_sc[...] = acc_sc[...] * factor + jnp.dot(
            p.astype(jnp.bfloat16), buf[slot, 1], preferred_element_type=jnp.float32
        )
        m_sc[...] = m_new
        return carry

    lax.fori_loop(0, n, body, 0)
    o_ref[...] = (acc_sc[...] / l_sc[...]).astype(o_ref.dtype)


def attend(ids, counts, q, ks, vs, kv_all):
    req, rows, hd = q.shape
    slots = ids.shape[1]
    block_shape = kv_all.shape[1:]
    return pl.pallas_call(
        functools.partial(attend_kernel, slots),
        out_shape=jax.ShapeDtypeStruct((req, rows, hd), jnp.bfloat16),
        grid_spec=pltpu.PrefetchScalarGridSpec(
            num_scalar_prefetch=2,
            grid=(req,),
            in_specs=[
                pl.BlockSpec((None, rows, hd), lambda j, ids, cnt: (j, 0, 0)),
                pl.BlockSpec((None, SUFFIX, hd), lambda j, ids, cnt: (j, 0, 0)),
                pl.BlockSpec((None, SUFFIX, hd), lambda j, ids, cnt: (j, 0, 0)),
                pl.BlockSpec(memory_space=pl.ANY),
            ],
            out_specs=pl.BlockSpec((None, rows, hd), lambda j, ids, cnt: (j, 0, 0)),
            scratch_shapes=[
                pltpu.VMEM((N_BUF,) + block_shape, kv_all.dtype),
                pltpu.SemaphoreType.DMA((N_BUF,)),
                pltpu.VMEM((rows, 1), jnp.float32),
                pltpu.VMEM((rows, 1), jnp.float32),
                pltpu.VMEM((rows, hd), jnp.float32),
            ],
        ),
        compiler_params=pltpu.CompilerParams(dimension_semantics=("arbitrary",)),
    )(ids.reshape(-1), counts, q, ks, vs, kv_all)


def exchange_kernel(n, x_ref, o_ref, recv, send_sem, recv_sem):
    me = lax.axis_index("mem")
    grp = lax.axis_index("grp")
    barrier = pltpu.get_barrier_semaphore()
    for k in range(1, n):
        pl.semaphore_signal(barrier, inc=1, device_id=(grp, lax.rem(me + k, n)), device_id_type=MESH)
    pl.semaphore_wait(barrier, n - 1)
    copies = []
    for k in range(1, n):
        peer = lax.rem(me + k, n)
        copy = pltpu.make_async_remote_copy(
            src_ref=x_ref.at[peer],
            dst_ref=recv.at[k],
            send_sem=send_sem.at[k],
            recv_sem=recv_sem.at[k],
            device_id=(grp, peer),
            device_id_type=MESH,
        )
        copy.start()
        copies.append(copy)
    total = x_ref[me].astype(jnp.float32)
    for k in range(1, n):
        copies[k - 1].wait()
        total = total + recv[k].astype(jnp.float32)
    o_ref[...] = total.astype(o_ref.dtype)


def exchange_sum(x):
    n, rows, cols = x.shape
    return pl.pallas_call(
        functools.partial(exchange_kernel, n),
        out_shape=jax.ShapeDtypeStruct((rows, cols), x.dtype),
        in_specs=[pl.BlockSpec(memory_space=pltpu.VMEM)],
        out_specs=pl.BlockSpec(memory_space=pltpu.VMEM),
        scratch_shapes=[
            pltpu.VMEM((n, rows, cols), x.dtype),
            pltpu.SemaphoreType.DMA((n,)),
            pltpu.SemaphoreType.DMA((n,)),
        ],
        compiler_params=pltpu.CompilerParams(collective_id=0, has_side_effects=True),
    )(x)


def on_device(n_mem, queries, suffix_kv, prefix_kv, out_weight, node_blocks, root_of, mid_of):
    group_index = lax.axis_index("grp")
    head_index = lax.axis_index("mem")
    tokens_dev, heads_dev, head_dim = queries.shape
    req_local = tokens_dev // SUFFIX
    group_size = QH // KVH
    kv_start = head_index * heads_dev // group_size
    prefix_part = lax.dynamic_index_in_dim(prefix_kv, kv_start, 3, keepdims=False)
    suffix_part = lax.dynamic_index_in_dim(suffix_kv, kv_start, 2, keepdims=False)
    kv_all = lax.all_gather(prefix_part, "grp", axis=0, tiled=True)

    request_ids = group_index * req_local + jnp.arange(req_local)
    ids, counts = path_table(request_ids, node_blocks, root_of, mid_of)

    q = queries.reshape(req_local, SUFFIX, heads_dev, head_dim).transpose(0, 2, 1, 3)
    q = q.reshape(req_local, heads_dev * SUFFIX, head_dim)
    ks = suffix_part[:, 0].reshape(req_local, SUFFIX, head_dim)
    vs = suffix_part[:, 1].reshape(req_local, SUFFIX, head_dim)
    attended = attend(ids, counts, q, ks, vs, kv_all)
    attended = attended.reshape(req_local, heads_dev, SUFFIX, head_dim)
    w = out_weight.reshape(heads_dev, head_dim, out_weight.shape[1])
    partial = lax.dot_general(
        attended, w, (((1, 3), (0, 1)), ((), ())), preferred_element_type=jnp.float32
    ).astype(jnp.bfloat16)
    partial = partial.reshape(tokens_dev, out_weight.shape[1])
    partial = partial.reshape(n_mem, tokens_dev // n_mem, out_weight.shape[1])
    return exchange_sum(partial)


def solution(mesh):
    return jax.shard_map(
        functools.partial(on_device, mesh.shape["mem"]),
        mesh=mesh,
        in_specs=(
            P("grp", "mem", None),
            P("grp", None, None, None),
            P("grp", None, None, None, None),
            P("mem", None),
            P(),
            P(),
            P(),
        ),
        out_specs=P(("grp", "mem"), None),
        check_vma=False,
    )
```

```python
import functools

import jax
import jax.numpy as jnp
from jax import lax
from jax.experimental import pallas as pl
from jax.experimental.pallas import tpu as pltpu
from jax.sharding import PartitionSpec as P

QH = 32
KVH = 4
SUFFIX = 256
MOST_BLK = 32
GROUP = 4
NEG = -1e30
MESH = pl.DeviceIdType.MESH


def path_table(request_ids, node_blocks, root_of, mid_of):
    nodes_all = node_blocks.shape[0]
    middles_all = root_of.shape[0]
    leaves = mid_of.shape[0]
    roots_all = nodes_all - middles_all - leaves
    firsts = jnp.cumsum(node_blocks) - node_blocks
    middles = jnp.sum(
        jnp.where(jnp.arange(leaves)[None, :] == request_ids[:, None], mid_of[None, :], 0), axis=1
    )
    root_ids = jnp.sum(
        jnp.where(jnp.arange(middles_all)[None, :] == middles[:, None], root_of[None, :], 0), axis=1
    )
    path_nodes = jnp.stack(
        [root_ids, roots_all + middles, roots_all + middles_all + request_ids], axis=1
    )
    picked = jnp.arange(nodes_all)[None, None, :] == path_nodes[:, :, None]
    starts = jnp.sum(jnp.where(picked, firsts[None, None, :], 0), axis=2)
    counts = jnp.sum(jnp.where(picked, node_blocks[None, None, :], 0), axis=2)
    ends = jnp.cumsum(counts, axis=1)
    begins = ends - counts
    slots = jnp.arange(3 * MOST_BLK)[None, :]
    which = (slots >= ends[:, 0:1]).astype(jnp.int32) + (slots >= ends[:, 1:2]).astype(jnp.int32)
    which = jnp.minimum(which, 2)
    pick = jnp.arange(3)[None, None, :] == which[:, :, None]
    start_of = jnp.sum(jnp.where(pick, starts[:, None, :], 0), axis=2)
    begin_of = jnp.sum(jnp.where(pick, begins[:, None, :], 0), axis=2)
    ids = start_of + slots - begin_of
    total = ends[:, 2]
    ids = jnp.where(slots < total[:, None], ids, 0)
    return ids.astype(jnp.int32), total.astype(jnp.int32)


def attend_kernel(slots, ids_ref, cnt_ref, q_ref, ks_ref, vs_ref, kv_hbm, o_ref, kbuf, vbuf, sem, m_sc, l_sc, acc_sc):
    j = pl.program_id(0)
    n = cnt_ref[j]
    rows, hd = q_ref.shape
    scale = hd ** (-0.5)
    contract = (((1,), (1,)), ((), ()))
    q = q_ref[...]

    scores = lax.dot_general(q, ks_ref[...], contract, preferred_element_type=jnp.float32) * scale
    tok = lax.broadcasted_iota(jnp.int32, scores.shape, 0) % SUFFIX
    key = lax.broadcasted_iota(jnp.int32, scores.shape, 1)
    scores = jnp.where(key <= tok, scores, NEG)
    high = jnp.max(scores, axis=-1, keepdims=True)
    weights = jnp.exp(scores - high)
    m_sc[...] = high
    l_sc[...] = jnp.sum(weights, axis=-1, keepdims=True)
    acc_sc[...] = jnp.dot(weights.astype(jnp.bfloat16), vs_ref[...], preferred_element_type=jnp.float32)

    rows_blk = kbuf.shape[1] // GROUP
    steps = (n + GROUP - 1) // GROUP

    def copies(step, slot, fresh):
        for g in range(GROUP):
            bid = ids_ref[j * slots + step * GROUP + g] if fresh else 0
            for half, dst in ((0, kbuf), (1, vbuf)):
                yield pltpu.make_async_copy(
                    kv_hbm.at[bid, half],
                    dst.at[slot, pl.ds(g * rows_blk, rows_blk)],
                    sem.at[slot, g, half],
                )

    def fetch(step, slot):
        for c in copies(step, slot, True):
            c.start()

    @pl.when(steps > 0)
    def _():
        fetch(0, 0)

    def body(st, carry):
        slot = st % 2
        for c in copies(st, slot, False):
            c.wait()

        @pl.when(st + 1 < steps)
        def _():
            fetch(st + 1, 1 - slot)

        s = lax.dot_general(q, kbuf[slot], contract, preferred_element_type=jnp.float32) * scale
        col = lax.broadcasted_iota(jnp.int32, s.shape, 1)
        s = jnp.where(col < (n - st * GROUP) * rows_blk, s, NEG)
        m_old = m_sc[...]
        m_new = jnp.maximum(m_old, jnp.max(s, axis=-1, keepdims=True))
        factor = jnp.exp(m_old - m_new)
        p = jnp.exp(s - m_new)
        l_sc[...] = l_sc[...] * factor + jnp.sum(p, axis=-1, keepdims=True)
        acc_sc[...] = acc_sc[...] * factor + jnp.dot(
            p.astype(jnp.bfloat16), vbuf[slot], preferred_element_type=jnp.float32
        )
        m_sc[...] = m_new
        return carry

    lax.fori_loop(0, steps, body, 0)
    o_ref[...] = (acc_sc[...] / l_sc[...]).astype(o_ref.dtype)


def attend(ids, counts, q, ks, vs, kv_all):
    req, rows, hd = q.shape
    slots = ids.shape[1]
    block_shape = kv_all.shape[1:]
    return pl.pallas_call(
        functools.partial(attend_kernel, slots),
        out_shape=jax.ShapeDtypeStruct((req, rows, hd), jnp.bfloat16),
        grid_spec=pltpu.PrefetchScalarGridSpec(
            num_scalar_prefetch=2,
            grid=(req,),
            in_specs=[
                pl.BlockSpec((None, rows, hd), lambda j, ids, cnt: (j, 0, 0)),
                pl.BlockSpec((None, SUFFIX, hd), lambda j, ids, cnt: (j, 0, 0)),
                pl.BlockSpec((None, SUFFIX, hd), lambda j, ids, cnt: (j, 0, 0)),
                pl.BlockSpec(memory_space=pl.ANY),
            ],
            out_specs=pl.BlockSpec((None, rows, hd), lambda j, ids, cnt: (j, 0, 0)),
            scratch_shapes=[
                pltpu.VMEM((2, GROUP * block_shape[1], block_shape[2]), kv_all.dtype),
                pltpu.VMEM((2, GROUP * block_shape[1], block_shape[2]), kv_all.dtype),
                pltpu.SemaphoreType.DMA((2, GROUP, 2)),
                pltpu.VMEM((rows, 1), jnp.float32),
                pltpu.VMEM((rows, 1), jnp.float32),
                pltpu.VMEM((rows, hd), jnp.float32),
            ],
        ),
        compiler_params=pltpu.CompilerParams(dimension_semantics=("arbitrary",)),
    )(ids.reshape(-1), counts, q, ks, vs, kv_all)


def exchange_kernel(n, x_ref, o_ref, recv, send_sem, recv_sem):
    me = lax.axis_index("mem")
    grp = lax.axis_index("grp")
    barrier = pltpu.get_barrier_semaphore()
    for k in range(1, n):
        pl.semaphore_signal(barrier, inc=1, device_id=(grp, lax.rem(me + k, n)), device_id_type=MESH)
    pl.semaphore_wait(barrier, n - 1)
    copies = []
    for k in range(1, n):
        peer = lax.rem(me + k, n)
        copy = pltpu.make_async_remote_copy(
            src_ref=x_ref.at[peer],
            dst_ref=recv.at[k],
            send_sem=send_sem.at[k],
            recv_sem=recv_sem.at[k],
            device_id=(grp, peer),
            device_id_type=MESH,
        )
        copy.start()
        copies.append(copy)
    total = x_ref[me].astype(jnp.float32)
    for k in range(1, n):
        copies[k - 1].wait()
        total = total + recv[k].astype(jnp.float32)
    o_ref[...] = total.astype(o_ref.dtype)


def exchange_sum(x):
    n, rows, cols = x.shape
    return pl.pallas_call(
        functools.partial(exchange_kernel, n),
        out_shape=jax.ShapeDtypeStruct((rows, cols), x.dtype),
        in_specs=[pl.BlockSpec(memory_space=pltpu.VMEM)],
        out_specs=pl.BlockSpec(memory_space=pltpu.VMEM),
        scratch_shapes=[
            pltpu.VMEM((n, rows, cols), x.dtype),
            pltpu.SemaphoreType.DMA((n,)),
            pltpu.SemaphoreType.DMA((n,)),
        ],
        compiler_params=pltpu.CompilerParams(collective_id=0, has_side_effects=True),
    )(x)


def on_device(n_mem, queries, suffix_kv, prefix_kv, out_weight, node_blocks, root_of, mid_of):
    group_index = lax.axis_index("grp")
    head_index = lax.axis_index("mem")
    tokens_dev, heads_dev, head_dim = queries.shape
    req_local = tokens_dev // SUFFIX
    group_size = QH // KVH
    kv_start = head_index * heads_dev // group_size
    prefix_part = lax.dynamic_index_in_dim(prefix_kv, kv_start, 3, keepdims=False)
    suffix_part = lax.dynamic_index_in_dim(suffix_kv, kv_start, 2, keepdims=False)
    kv_all = lax.all_gather(prefix_part, "grp", axis=0, tiled=True)

    request_ids = group_index * req_local + jnp.arange(req_local)
    ids, counts = path_table(request_ids, node_blocks, root_of, mid_of)

    q = queries.reshape(req_local, SUFFIX, heads_dev, head_dim).transpose(0, 2, 1, 3)
    q = q.reshape(req_local, heads_dev * SUFFIX, head_dim)
    ks = suffix_part[:, 0].reshape(req_local, SUFFIX, head_dim)
    vs = suffix_part[:, 1].reshape(req_local, SUFFIX, head_dim)
    attended = attend(ids, counts, q, ks, vs, kv_all)
    attended = attended.reshape(req_local, heads_dev, SUFFIX, head_dim)
    w = out_weight.reshape(heads_dev, head_dim, out_weight.shape[1])
    partial = lax.dot_general(
        attended, w, (((1, 3), (0, 1)), ((), ())), preferred_element_type=jnp.float32
    ).astype(jnp.bfloat16)
    partial = partial.reshape(tokens_dev, out_weight.shape[1])
    partial = partial.reshape(n_mem, tokens_dev // n_mem, out_weight.shape[1])
    return exchange_sum(partial)


def solution(mesh):
    return jax.shard_map(
        functools.partial(on_device, mesh.shape["mem"]),
        mesh=mesh,
        in_specs=(
            P("grp", "mem", None),
            P("grp", None, None, None),
            P("grp", None, None, None, None),
            P("mem", None),
            P(),
            P(),
            P(),
        ),
        out_specs=P(("grp", "mem"), None),
        check_vma=False,
    )
```

```python
import functools

import jax
import jax.numpy as jnp
from jax import lax
from jax.experimental import pallas as pl
from jax.experimental.pallas import tpu as pltpu
from jax.sharding import PartitionSpec as P

QH = 32
KVH = 4
SUFFIX = 256
MOST_BLK = 32
GROUP = 8
NEG = -1e30
MESH = pl.DeviceIdType.MESH


def path_table(request_ids, node_blocks, root_of, mid_of):
    nodes_all = node_blocks.shape[0]
    middles_all = root_of.shape[0]
    leaves = mid_of.shape[0]
    roots_all = nodes_all - middles_all - leaves
    firsts = jnp.cumsum(node_blocks) - node_blocks
    middles = jnp.sum(
        jnp.where(jnp.arange(leaves)[None, :] == request_ids[:, None], mid_of[None, :], 0), axis=1
    )
    root_ids = jnp.sum(
        jnp.where(jnp.arange(middles_all)[None, :] == middles[:, None], root_of[None, :], 0), axis=1
    )
    path_nodes = jnp.stack(
        [root_ids, roots_all + middles, roots_all + middles_all + request_ids], axis=1
    )
    picked = jnp.arange(nodes_all)[None, None, :] == path_nodes[:, :, None]
    starts = jnp.sum(jnp.where(picked, firsts[None, None, :], 0), axis=2)
    counts = jnp.sum(jnp.where(picked, node_blocks[None, None, :], 0), axis=2)
    ends = jnp.cumsum(counts, axis=1)
    begins = ends - counts
    slots = jnp.arange(3 * MOST_BLK)[None, :]
    which = (slots >= ends[:, 0:1]).astype(jnp.int32) + (slots >= ends[:, 1:2]).astype(jnp.int32)
    which = jnp.minimum(which, 2)
    pick = jnp.arange(3)[None, None, :] == which[:, :, None]
    start_of = jnp.sum(jnp.where(pick, starts[:, None, :], 0), axis=2)
    begin_of = jnp.sum(jnp.where(pick, begins[:, None, :], 0), axis=2)
    ids = start_of + slots - begin_of
    total = ends[:, 2]
    ids = jnp.where(slots < total[:, None], ids, 0)
    return ids.astype(jnp.int32), total.astype(jnp.int32)


def attend_kernel(slots, ids_ref, cnt_ref, q_ref, ks_ref, vs_ref, kv_hbm, o_ref, kbuf, vbuf, sem, m_sc, l_sc, acc_sc):
    j = pl.program_id(0)
    n = cnt_ref[j]
    rows, hd = q_ref.shape
    scale = hd ** (-0.5)
    contract = (((1,), (1,)), ((), ()))
    q = q_ref[...]

    scores = lax.dot_general(q, ks_ref[...], contract, preferred_element_type=jnp.float32) * scale
    tok = lax.broadcasted_iota(jnp.int32, scores.shape, 0) % SUFFIX
    key = lax.broadcasted_iota(jnp.int32, scores.shape, 1)
    scores = jnp.where(key <= tok, scores, NEG)
    high = jnp.max(scores, axis=-1, keepdims=True)
    weights = jnp.exp(scores - high)
    m_sc[...] = high
    l_sc[...] = jnp.sum(weights, axis=-1, keepdims=True)
    acc_sc[...] = jnp.dot(weights.astype(jnp.bfloat16), vs_ref[...], preferred_element_type=jnp.float32)

    rows_blk = kbuf.shape[1] // GROUP
    steps = (n + GROUP - 1) // GROUP

    def copies(step, slot, fresh):
        for g in range(GROUP):
            bid = ids_ref[j * slots + step * GROUP + g] if fresh else 0
            for half, dst in ((0, kbuf), (1, vbuf)):
                yield pltpu.make_async_copy(
                    kv_hbm.at[bid, half],
                    dst.at[slot, pl.ds(g * rows_blk, rows_blk)],
                    sem.at[slot, g, half],
                )

    def fetch(step, slot):
        for c in copies(step, slot, True):
            c.start()

    @pl.when(steps > 0)
    def _():
        fetch(0, 0)

    def body(st, carry):
        slot = st % 2
        for c in copies(st, slot, False):
            c.wait()

        @pl.when(st + 1 < steps)
        def _():
            fetch(st + 1, 1 - slot)

        limit = (n - st * GROUP) * rows_blk

        def update(masked):
            s = lax.dot_general(q, kbuf[slot], contract, preferred_element_type=jnp.float32) * scale
            if masked:
                col = lax.broadcasted_iota(jnp.int32, s.shape, 1)
                s = jnp.where(col < limit, s, NEG)
            m_old = m_sc[...]
            m_new = jnp.maximum(m_old, jnp.max(s, axis=-1, keepdims=True))
            factor = jnp.exp(m_old - m_new)
            p = jnp.exp(s - m_new)
            l_sc[...] = l_sc[...] * factor + jnp.sum(p, axis=-1, keepdims=True)
            acc_sc[...] = acc_sc[...] * factor + jnp.dot(
                p.astype(jnp.bfloat16), vbuf[slot], preferred_element_type=jnp.float32
            )
            m_sc[...] = m_new

        @pl.when(limit >= kbuf.shape[1])
        def _():
            update(False)

        @pl.when(limit < kbuf.shape[1])
        def _():
            update(True)

        return carry

    lax.fori_loop(0, steps, body, 0)
    o_ref[...] = (acc_sc[...] / l_sc[...]).astype(o_ref.dtype)


def attend(ids, counts, q, ks, vs, kv_all):
    req, rows, hd = q.shape
    slots = ids.shape[1]
    block_shape = kv_all.shape[1:]
    return pl.pallas_call(
        functools.partial(attend_kernel, slots),
        out_shape=jax.ShapeDtypeStruct((req, rows, hd), jnp.bfloat16),
        grid_spec=pltpu.PrefetchScalarGridSpec(
            num_scalar_prefetch=2,
            grid=(req,),
            in_specs=[
                pl.BlockSpec((None, rows, hd), lambda j, ids, cnt: (j, 0, 0)),
                pl.BlockSpec((None, SUFFIX, hd), lambda j, ids, cnt: (j, 0, 0)),
                pl.BlockSpec((None, SUFFIX, hd), lambda j, ids, cnt: (j, 0, 0)),
                pl.BlockSpec(memory_space=pl.ANY),
            ],
            out_specs=pl.BlockSpec((None, rows, hd), lambda j, ids, cnt: (j, 0, 0)),
            scratch_shapes=[
                pltpu.VMEM((2, GROUP * block_shape[1], block_shape[2]), kv_all.dtype),
                pltpu.VMEM((2, GROUP * block_shape[1], block_shape[2]), kv_all.dtype),
                pltpu.SemaphoreType.DMA((2, GROUP, 2)),
                pltpu.VMEM((rows, 1), jnp.float32),
                pltpu.VMEM((rows, 1), jnp.float32),
                pltpu.VMEM((rows, hd), jnp.float32),
            ],
        ),
        compiler_params=pltpu.CompilerParams(dimension_semantics=("arbitrary",)),
    )(ids.reshape(-1), counts, q, ks, vs, kv_all)


def exchange_kernel(n, x_ref, o_ref, recv, send_sem, recv_sem):
    me = lax.axis_index("mem")
    grp = lax.axis_index("grp")
    barrier = pltpu.get_barrier_semaphore()
    for k in range(1, n):
        pl.semaphore_signal(barrier, inc=1, device_id=(grp, lax.rem(me + k, n)), device_id_type=MESH)
    pl.semaphore_wait(barrier, n - 1)
    copies = []
    for k in range(1, n):
        peer = lax.rem(me + k, n)
        copy = pltpu.make_async_remote_copy(
            src_ref=x_ref.at[peer],
            dst_ref=recv.at[k],
            send_sem=send_sem.at[k],
            recv_sem=recv_sem.at[k],
            device_id=(grp, peer),
            device_id_type=MESH,
        )
        copy.start()
        copies.append(copy)
    total = x_ref[me].astype(jnp.float32)
    for k in range(1, n):
        copies[k - 1].wait()
        total = total + recv[k].astype(jnp.float32)
    o_ref[...] = total.astype(o_ref.dtype)


def exchange_sum(x):
    n, rows, cols = x.shape
    return pl.pallas_call(
        functools.partial(exchange_kernel, n),
        out_shape=jax.ShapeDtypeStruct((rows, cols), x.dtype),
        in_specs=[pl.BlockSpec(memory_space=pltpu.VMEM)],
        out_specs=pl.BlockSpec(memory_space=pltpu.VMEM),
        scratch_shapes=[
            pltpu.VMEM((n, rows, cols), x.dtype),
            pltpu.SemaphoreType.DMA((n,)),
            pltpu.SemaphoreType.DMA((n,)),
        ],
        compiler_params=pltpu.CompilerParams(collective_id=0, has_side_effects=True),
    )(x)


def on_device(n_mem, queries, suffix_kv, prefix_kv, out_weight, node_blocks, root_of, mid_of):
    group_index = lax.axis_index("grp")
    head_index = lax.axis_index("mem")
    tokens_dev, heads_dev, head_dim = queries.shape
    req_local = tokens_dev // SUFFIX
    group_size = QH // KVH
    kv_start = head_index * heads_dev // group_size
    prefix_part = lax.dynamic_index_in_dim(prefix_kv, kv_start, 3, keepdims=False)
    suffix_part = lax.dynamic_index_in_dim(suffix_kv, kv_start, 2, keepdims=False)
    kv_all = lax.all_gather(prefix_part, "grp", axis=0, tiled=True)

    request_ids = group_index * req_local + jnp.arange(req_local)
    ids, counts = path_table(request_ids, node_blocks, root_of, mid_of)

    q = queries.reshape(req_local, SUFFIX, heads_dev, head_dim).transpose(0, 2, 1, 3)
    q = q.reshape(req_local, heads_dev * SUFFIX, head_dim)
    ks = suffix_part[:, 0].reshape(req_local, SUFFIX, head_dim)
    vs = suffix_part[:, 1].reshape(req_local, SUFFIX, head_dim)
    attended = attend(ids, counts, q, ks, vs, kv_all)
    attended = attended.reshape(req_local, heads_dev, SUFFIX, head_dim)
    w = out_weight.reshape(heads_dev, head_dim, out_weight.shape[1])
    partial = lax.dot_general(
        attended, w, (((1, 3), (0, 1)), ((), ())), preferred_element_type=jnp.float32
    ).astype(jnp.bfloat16)
    partial = partial.reshape(tokens_dev, out_weight.shape[1])
    partial = partial.reshape(n_mem, tokens_dev // n_mem, out_weight.shape[1])
    return exchange_sum(partial)


def solution(mesh):
    return jax.shard_map(
        functools.partial(on_device, mesh.shape["mem"]),
        mesh=mesh,
        in_specs=(
            P("grp", "mem", None),
            P("grp", None, None, None),
            P("grp", None, None, None, None),
            P("mem", None),
            P(),
            P(),
            P(),
        ),
        out_specs=P(("grp", "mem"), None),
        check_vma=False,
    )
```

```python
import functools

import jax
import jax.numpy as jnp
from jax import lax
from jax.experimental import pallas as pl
from jax.experimental.pallas import tpu as pltpu
from jax.sharding import Mesh, PartitionSpec as P

QH = 32
KVH = 4
SUFFIX = 256
MOST_BLK = 32
GROUP = 8
NEG = -1e30
MESH = pl.DeviceIdType.MESH


def path_table(request_ids, node_blocks, root_of, mid_of):
    nodes_all = node_blocks.shape[0]
    middles_all = root_of.shape[0]
    leaves = mid_of.shape[0]
    roots_all = nodes_all - middles_all - leaves
    firsts = jnp.cumsum(node_blocks) - node_blocks
    middles = jnp.sum(
        jnp.where(jnp.arange(leaves)[None, :] == request_ids[:, None], mid_of[None, :], 0), axis=1
    )
    root_ids = jnp.sum(
        jnp.where(jnp.arange(middles_all)[None, :] == middles[:, None], root_of[None, :], 0), axis=1
    )
    path_nodes = jnp.stack(
        [root_ids, roots_all + middles, roots_all + middles_all + request_ids], axis=1
    )
    picked = jnp.arange(nodes_all)[None, None, :] == path_nodes[:, :, None]
    starts = jnp.sum(jnp.where(picked, firsts[None, None, :], 0), axis=2)
    counts = jnp.sum(jnp.where(picked, node_blocks[None, None, :], 0), axis=2)
    ends = jnp.cumsum(counts, axis=1)
    begins = ends - counts
    slots = jnp.arange(3 * MOST_BLK)[None, :]
    which = (slots >= ends[:, 0:1]).astype(jnp.int32) + (slots >= ends[:, 1:2]).astype(jnp.int32)
    which = jnp.minimum(which, 2)
    pick = jnp.arange(3)[None, None, :] == which[:, :, None]
    start_of = jnp.sum(jnp.where(pick, starts[:, None, :], 0), axis=2)
    begin_of = jnp.sum(jnp.where(pick, begins[:, None, :], 0), axis=2)
    ids = start_of + slots - begin_of
    total = ends[:, 2]
    ids = jnp.where(slots < total[:, None], ids, 0)
    return ids.astype(jnp.int32), total.astype(jnp.int32)


def attend_kernel(slots, ids_ref, cnt_ref, q_ref, ks_ref, vs_ref, kv_hbm, o_ref, kbuf, vbuf, sem, m_sc, l_sc, acc_sc):
    j = pl.program_id(0)
    n = cnt_ref[j]
    rows, hd = q_ref.shape
    scale = hd ** (-0.5)
    contract = (((1,), (1,)), ((), ()))
    q = q_ref[...]

    scores = lax.dot_general(q, ks_ref[...], contract, preferred_element_type=jnp.float32) * scale
    tok = lax.broadcasted_iota(jnp.int32, scores.shape, 0) % SUFFIX
    key = lax.broadcasted_iota(jnp.int32, scores.shape, 1)
    scores = jnp.where(key <= tok, scores, NEG)
    high = jnp.max(scores, axis=-1, keepdims=True)
    weights = jnp.exp(scores - high)
    m_sc[...] = high
    l_sc[...] = jnp.sum(weights, axis=-1, keepdims=True)
    acc_sc[...] = jnp.dot(weights.astype(jnp.bfloat16), vs_ref[...], preferred_element_type=jnp.float32)

    rows_blk = kbuf.shape[1] // GROUP
    steps = (n + GROUP - 1) // GROUP

    def copies(step, slot, fresh):
        for g in range(GROUP):
            bid = ids_ref[j * slots + step * GROUP + g] if fresh else 0
            for half, dst in ((0, kbuf), (1, vbuf)):
                yield pltpu.make_async_copy(
                    kv_hbm.at[bid, half],
                    dst.at[slot, pl.ds(g * rows_blk, rows_blk)],
                    sem.at[slot, g, half],
                )

    def fetch(step, slot):
        for c in copies(step, slot, True):
            c.start()

    @pl.when(steps > 0)
    def _():
        fetch(0, 0)

    def body(st, carry):
        slot = st % 2
        for c in copies(st, slot, False):
            c.wait()

        @pl.when(st + 1 < steps)
        def _():
            fetch(st + 1, 1 - slot)

        limit = (n - st * GROUP) * rows_blk

        def update(masked):
            s = lax.dot_general(q, kbuf[slot], contract, preferred_element_type=jnp.float32) * scale
            if masked:
                col = lax.broadcasted_iota(jnp.int32, s.shape, 1)
                s = jnp.where(col < limit, s, NEG)
            m_old = m_sc[...]
            m_new = jnp.maximum(m_old, jnp.max(s, axis=-1, keepdims=True))
            factor = jnp.exp(m_old - m_new)
            p = jnp.exp(s - m_new)
            l_sc[...] = l_sc[...] * factor + jnp.sum(p, axis=-1, keepdims=True)
            acc_sc[...] = acc_sc[...] * factor + jnp.dot(
                p.astype(jnp.bfloat16), vbuf[slot], preferred_element_type=jnp.float32
            )
            m_sc[...] = m_new

        @pl.when(limit >= kbuf.shape[1])
        def _():
            update(False)

        @pl.when(limit < kbuf.shape[1])
        def _():
            update(True)

        return carry

    lax.fori_loop(0, steps, body, 0)
    o_ref[...] = (acc_sc[...] / l_sc[...]).astype(o_ref.dtype)


def attend(ids, counts, q, ks, vs, kv_all):
    req, rows, hd = q.shape
    slots = ids.shape[1]
    block_shape = kv_all.shape[1:]
    return pl.pallas_call(
        functools.partial(attend_kernel, slots),
        out_shape=jax.ShapeDtypeStruct((req, rows, hd), jnp.bfloat16),
        grid_spec=pltpu.PrefetchScalarGridSpec(
            num_scalar_prefetch=2,
            grid=(req,),
            in_specs=[
                pl.BlockSpec((None, rows, hd), lambda j, ids, cnt: (j, 0, 0)),
                pl.BlockSpec((None, SUFFIX, hd), lambda j, ids, cnt: (j, 0, 0)),
                pl.BlockSpec((None, SUFFIX, hd), lambda j, ids, cnt: (j, 0, 0)),
                pl.BlockSpec(memory_space=pl.ANY),
            ],
            out_specs=pl.BlockSpec((None, rows, hd), lambda j, ids, cnt: (j, 0, 0)),
            scratch_shapes=[
                pltpu.VMEM((2, GROUP * block_shape[1], block_shape[2]), kv_all.dtype),
                pltpu.VMEM((2, GROUP * block_shape[1], block_shape[2]), kv_all.dtype),
                pltpu.SemaphoreType.DMA((2, GROUP, 2)),
                pltpu.VMEM((rows, 1), jnp.float32),
                pltpu.VMEM((rows, 1), jnp.float32),
                pltpu.VMEM((rows, hd), jnp.float32),
            ],
        ),
        compiler_params=pltpu.CompilerParams(dimension_semantics=("arbitrary",)),
    )(ids.reshape(-1), counts, q, ks, vs, kv_all)


def exchange_kernel(n, x_ref, o_ref, recv, send_sem, recv_sem):
    me = lax.axis_index("mem")
    grp = (lax.axis_index("xl"), lax.axis_index("zc"))
    barrier = pltpu.get_barrier_semaphore()
    for k in range(1, n):
        pl.semaphore_signal(barrier, inc=1, device_id=grp + (lax.rem(me + k, n),), device_id_type=MESH)
    pl.semaphore_wait(barrier, n - 1)
    copies = []
    for k in range(1, n):
        peer = lax.rem(me + k, n)
        copy = pltpu.make_async_remote_copy(
            src_ref=x_ref.at[peer],
            dst_ref=recv.at[k],
            send_sem=send_sem.at[k],
            recv_sem=recv_sem.at[k],
            device_id=grp + (peer,),
            device_id_type=MESH,
        )
        copy.start()
        copies.append(copy)
    total = x_ref[me].astype(jnp.float32)
    for k in range(1, n):
        copies[k - 1].wait()
        total = total + recv[k].astype(jnp.float32)
    o_ref[...] = total.astype(o_ref.dtype)


def exchange_sum(x):
    n, rows, cols = x.shape
    return pl.pallas_call(
        functools.partial(exchange_kernel, n),
        out_shape=jax.ShapeDtypeStruct((rows, cols), x.dtype),
        in_specs=[pl.BlockSpec(memory_space=pltpu.VMEM)],
        out_specs=pl.BlockSpec(memory_space=pltpu.VMEM),
        scratch_shapes=[
            pltpu.VMEM((n, rows, cols), x.dtype),
            pltpu.SemaphoreType.DMA((n,)),
            pltpu.SemaphoreType.DMA((n,)),
        ],
        compiler_params=pltpu.CompilerParams(collective_id=0, has_side_effects=True),
    )(x)


def on_device(n_mem, n_zc, queries, suffix_kv, prefix_kv, out_weight, node_blocks, root_of, mid_of):
    group_index = lax.axis_index("xl") * n_zc + lax.axis_index("zc")
    head_index = lax.axis_index("mem")
    tokens_dev, heads_dev, head_dim = queries.shape
    req_local = tokens_dev // SUFFIX
    group_size = QH // KVH
    kv_start = head_index * heads_dev // group_size
    prefix_part = lax.dynamic_index_in_dim(prefix_kv, kv_start, 3, keepdims=False)
    suffix_part = lax.dynamic_index_in_dim(suffix_kv, kv_start, 2, keepdims=False)
    own_blocks = prefix_part.shape[0]
    kv_pair = lax.all_gather(prefix_part, "xl", axis=0, tiled=True)
    kv_all = lax.all_gather(kv_pair, "zc", axis=0, tiled=True)

    request_ids = group_index * req_local + jnp.arange(req_local)
    ids, counts = path_table(request_ids, node_blocks, root_of, mid_of)
    owner = ids // own_blocks
    ids = (owner % n_zc) * kv_pair.shape[0] + (owner // n_zc) * own_blocks + ids % own_blocks

    q = queries.reshape(req_local, SUFFIX, heads_dev, head_dim).transpose(0, 2, 1, 3)
    q = q.reshape(req_local, heads_dev * SUFFIX, head_dim)
    ks = suffix_part[:, 0].reshape(req_local, SUFFIX, head_dim)
    vs = suffix_part[:, 1].reshape(req_local, SUFFIX, head_dim)
    attended = attend(ids, counts, q, ks, vs, kv_all)
    attended = attended.reshape(req_local, heads_dev, SUFFIX, head_dim)
    w = out_weight.reshape(heads_dev, head_dim, out_weight.shape[1])
    partial = lax.dot_general(
        attended, w, (((1, 3), (0, 1)), ((), ())), preferred_element_type=jnp.float32
    ).astype(jnp.bfloat16)
    partial = partial.reshape(tokens_dev, out_weight.shape[1])
    partial = partial.reshape(n_mem, tokens_dev // n_mem, out_weight.shape[1])
    return exchange_sum(partial)


def solution(mesh):
    n_xl = 2
    n_grp, n_mem = mesh.shape["grp"], mesh.shape["mem"]
    fine = Mesh(mesh.devices.reshape(n_xl, n_grp // n_xl, n_mem), ("xl", "zc", "mem"))
    grp = ("xl", "zc")
    return jax.shard_map(
        functools.partial(on_device, n_mem, n_grp // n_xl),
        mesh=fine,
        in_specs=(
            P(grp, "mem", None),
            P(grp, None, None, None),
            P(grp, None, None, None, None),
            P("mem", None),
            P(),
            P(),
            P(),
        ),
        out_specs=P(grp + ("mem",), None),
        check_vma=False,
    )
```

```python
import functools

import jax
import jax.numpy as jnp
from jax import lax
from jax.experimental import pallas as pl
from jax.experimental.pallas import tpu as pltpu
from jax.sharding import PartitionSpec as P

QH = 32
KVH = 4
SUFFIX = 256
MOST_BLK = 32
GROUP = 8
NEG = -1e30
MESH = pl.DeviceIdType.MESH


def path_table(request_ids, node_blocks, root_of, mid_of):
    nodes_all = node_blocks.shape[0]
    middles_all = root_of.shape[0]
    leaves = mid_of.shape[0]
    roots_all = nodes_all - middles_all - leaves
    firsts = jnp.cumsum(node_blocks) - node_blocks
    middles = jnp.sum(
        jnp.where(jnp.arange(leaves)[None, :] == request_ids[:, None], mid_of[None, :], 0), axis=1
    )
    root_ids = jnp.sum(
        jnp.where(jnp.arange(middles_all)[None, :] == middles[:, None], root_of[None, :], 0), axis=1
    )
    path_nodes = jnp.stack(
        [root_ids, roots_all + middles, roots_all + middles_all + request_ids], axis=1
    )
    picked = jnp.arange(nodes_all)[None, None, :] == path_nodes[:, :, None]
    starts = jnp.sum(jnp.where(picked, firsts[None, None, :], 0), axis=2)
    counts = jnp.sum(jnp.where(picked, node_blocks[None, None, :], 0), axis=2)
    ends = jnp.cumsum(counts, axis=1)
    begins = ends - counts
    slots = jnp.arange(3 * MOST_BLK)[None, :]
    which = (slots >= ends[:, 0:1]).astype(jnp.int32) + (slots >= ends[:, 1:2]).astype(jnp.int32)
    which = jnp.minimum(which, 2)
    pick = jnp.arange(3)[None, None, :] == which[:, :, None]
    start_of = jnp.sum(jnp.where(pick, starts[:, None, :], 0), axis=2)
    begin_of = jnp.sum(jnp.where(pick, begins[:, None, :], 0), axis=2)
    ids = start_of + slots - begin_of
    total = ends[:, 2]
    ids = jnp.where(slots < total[:, None], ids, 0)
    return ids.astype(jnp.int32), total.astype(jnp.int32)


def suffix_kernel(q_ref, ks_ref, vs_ref, m_ref, l_ref, acc_ref):
    hd = q_ref.shape[-1]
    contract = (((1,), (1,)), ((), ()))
    scores = lax.dot_general(q_ref[...], ks_ref[...], contract, preferred_element_type=jnp.float32)
    scores = scores * hd ** (-0.5)
    tok = lax.broadcasted_iota(jnp.int32, scores.shape, 0) % SUFFIX
    key = lax.broadcasted_iota(jnp.int32, scores.shape, 1)
    scores = jnp.where(key <= tok, scores, NEG)
    high = jnp.max(scores, axis=-1, keepdims=True)
    weights = jnp.exp(scores - high)
    m_ref[...] = high
    l_ref[...] = jnp.sum(weights, axis=-1, keepdims=True)
    acc_ref[...] = jnp.dot(weights.astype(jnp.bfloat16), vs_ref[...], preferred_element_type=jnp.float32)


def suffix_attend(q, ks, vs):
    req, rows, hd = q.shape
    index = lambda j: (j, 0, 0)
    return pl.pallas_call(
        suffix_kernel,
        out_shape=(
            jax.ShapeDtypeStruct((req, rows, 1), jnp.float32),
            jax.ShapeDtypeStruct((req, rows, 1), jnp.float32),
            jax.ShapeDtypeStruct((req, rows, hd), jnp.float32),
        ),
        grid=(req,),
        in_specs=[
            pl.BlockSpec((None, rows, hd), index),
            pl.BlockSpec((None, SUFFIX, hd), index),
            pl.BlockSpec((None, SUFFIX, hd), index),
        ],
        out_specs=[
            pl.BlockSpec((None, rows, 1), index),
            pl.BlockSpec((None, rows, 1), index),
            pl.BlockSpec((None, rows, hd), index),
        ],
        compiler_params=pltpu.CompilerParams(dimension_semantics=("arbitrary",)),
    )(q, ks, vs)


def attend_kernel(slots, ids_ref, cnt_ref, q_ref, m0_ref, l0_ref, acc0_ref, kv_hbm, o_ref, kbuf, vbuf, sem, m_sc, l_sc, acc_sc):
    j = pl.program_id(0)
    n = cnt_ref[j]
    rows, hd = q_ref.shape
    scale = hd ** (-0.5)
    contract = (((1,), (1,)), ((), ()))
    q = q_ref[...]
    m_sc[...] = m0_ref[...]
    l_sc[...] = l0_ref[...]
    acc_sc[...] = acc0_ref[...]

    rows_blk = kbuf.shape[1] // GROUP
    steps = (n + GROUP - 1) // GROUP

    def copies(step, slot, fresh):
        for g in range(GROUP):
            bid = ids_ref[j * slots + step * GROUP + g] if fresh else 0
            for half, dst in ((0, kbuf), (1, vbuf)):
                yield pltpu.make_async_copy(
                    kv_hbm.at[bid, half],
                    dst.at[slot, pl.ds(g * rows_blk, rows_blk)],
                    sem.at[slot, g, half],
                )

    def fetch(step, slot):
        for c in copies(step, slot, True):
            c.start()

    @pl.when(steps > 0)
    def _():
        fetch(0, 0)

    def body(st, carry):
        slot = st % 2
        for c in copies(st, slot, False):
            c.wait()

        @pl.when(st + 1 < steps)
        def _():
            fetch(st + 1, 1 - slot)

        limit = (n - st * GROUP) * rows_blk

        def update(masked):
            s = lax.dot_general(q, kbuf[slot], contract, preferred_element_type=jnp.float32) * scale
            if masked:
                col = lax.broadcasted_iota(jnp.int32, s.shape, 1)
                s = jnp.where(col < limit, s, NEG)
            m_old = m_sc[...]
            m_new = jnp.maximum(m_old, jnp.max(s, axis=-1, keepdims=True))
            factor = jnp.exp(m_old - m_new)
            p = jnp.exp(s - m_new)
            l_sc[...] = l_sc[...] * factor + jnp.sum(p, axis=-1, keepdims=True)
            acc_sc[...] = acc_sc[...] * factor + jnp.dot(
                p.astype(jnp.bfloat16), vbuf[slot], preferred_element_type=jnp.float32
            )
            m_sc[...] = m_new

        @pl.when(limit >= kbuf.shape[1])
        def _():
            update(False)

        @pl.when(limit < kbuf.shape[1])
        def _():
            update(True)

        return carry

    lax.fori_loop(0, steps, body, 0)
    o_ref[...] = (acc_sc[...] / l_sc[...]).astype(o_ref.dtype)


def attend(ids, counts, q, state, kv_all):
    req, rows, hd = q.shape
    slots = ids.shape[1]
    block_shape = kv_all.shape[1:]
    return pl.pallas_call(
        functools.partial(attend_kernel, slots),
        out_shape=jax.ShapeDtypeStruct((req, rows, hd), jnp.bfloat16),
        grid_spec=pltpu.PrefetchScalarGridSpec(
            num_scalar_prefetch=2,
            grid=(req,),
            in_specs=[
                pl.BlockSpec((None, rows, hd), lambda j, ids, cnt: (j, 0, 0)),
                pl.BlockSpec((None, rows, 1), lambda j, ids, cnt: (j, 0, 0)),
                pl.BlockSpec((None, rows, 1), lambda j, ids, cnt: (j, 0, 0)),
                pl.BlockSpec((None, rows, hd), lambda j, ids, cnt: (j, 0, 0)),
                pl.BlockSpec(memory_space=pl.ANY),
            ],
            out_specs=pl.BlockSpec((None, rows, hd), lambda j, ids, cnt: (j, 0, 0)),
            scratch_shapes=[
                pltpu.VMEM((2, GROUP * block_shape[1], block_shape[2]), kv_all.dtype),
                pltpu.VMEM((2, GROUP * block_shape[1], block_shape[2]), kv_all.dtype),
                pltpu.SemaphoreType.DMA((2, GROUP, 2)),
                pltpu.VMEM((rows, 1), jnp.float32),
                pltpu.VMEM((rows, 1), jnp.float32),
                pltpu.VMEM((rows, hd), jnp.float32),
            ],
        ),
        compiler_params=pltpu.CompilerParams(dimension_semantics=("arbitrary",)),
    )(ids.reshape(-1), counts, q, *state, kv_all)


def exchange_kernel(n, x_ref, o_ref, recv, send_sem, recv_sem):
    me = lax.axis_index("mem")
    grp = lax.axis_index("grp")
    barrier = pltpu.get_barrier_semaphore()
    for k in range(1, n):
        pl.semaphore_signal(barrier, inc=1, device_id=(grp, lax.rem(me + k, n)), device_id_type=MESH)
    pl.semaphore_wait(barrier, n - 1)
    copies = []
    for k in range(1, n):
        peer = lax.rem(me + k, n)
        copy = pltpu.make_async_remote_copy(
            src_ref=x_ref.at[peer],
            dst_ref=recv.at[k],
            send_sem=send_sem.at[k],
            recv_sem=recv_sem.at[k],
            device_id=(grp, peer),
            device_id_type=MESH,
        )
        copy.start()
        copies.append(copy)
    total = x_ref[me].astype(jnp.float32)
    for k in range(1, n):
        copies[k - 1].wait()
        total = total + recv[k].astype(jnp.float32)
    o_ref[...] = total.astype(o_ref.dtype)


def exchange_sum(x):
    n, rows, cols = x.shape
    return pl.pallas_call(
        functools.partial(exchange_kernel, n),
        out_shape=jax.ShapeDtypeStruct((rows, cols), x.dtype),
        in_specs=[pl.BlockSpec(memory_space=pltpu.VMEM)],
        out_specs=pl.BlockSpec(memory_space=pltpu.VMEM),
        scratch_shapes=[
            pltpu.VMEM((n, rows, cols), x.dtype),
            pltpu.SemaphoreType.DMA((n,)),
            pltpu.SemaphoreType.DMA((n,)),
        ],
        compiler_params=pltpu.CompilerParams(collective_id=0, has_side_effects=True),
    )(x)


def on_device(n_mem, queries, suffix_kv, prefix_kv, out_weight, node_blocks, root_of, mid_of):
    group_index = lax.axis_index("grp")
    head_index = lax.axis_index("mem")
    tokens_dev, heads_dev, head_dim = queries.shape
    req_local = tokens_dev // SUFFIX
    group_size = QH // KVH
    kv_start = head_index * heads_dev // group_size
    prefix_part = lax.dynamic_index_in_dim(prefix_kv, kv_start, 3, keepdims=False)
    suffix_part = lax.dynamic_index_in_dim(suffix_kv, kv_start, 2, keepdims=False)
    kv_all = lax.all_gather(prefix_part, "grp", axis=0, tiled=True)

    request_ids = group_index * req_local + jnp.arange(req_local)
    ids, counts = path_table(request_ids, node_blocks, root_of, mid_of)

    q = queries.reshape(req_local, SUFFIX, heads_dev, head_dim).transpose(0, 2, 1, 3)
    q = q.reshape(req_local, heads_dev * SUFFIX, head_dim)
    ks = suffix_part[:, 0].reshape(req_local, SUFFIX, head_dim)
    vs = suffix_part[:, 1].reshape(req_local, SUFFIX, head_dim)
    attended = attend(ids, counts, q, suffix_attend(q, ks, vs), kv_all)
    attended = attended.reshape(req_local, heads_dev, SUFFIX, head_dim)
    w = out_weight.reshape(heads_dev, head_dim, out_weight.shape[1])
    partial = lax.dot_general(
        attended, w, (((1, 3), (0, 1)), ((), ())), preferred_element_type=jnp.float32
    ).astype(jnp.bfloat16)
    partial = partial.reshape(tokens_dev, out_weight.shape[1])
    partial = partial.reshape(n_mem, tokens_dev // n_mem, out_weight.shape[1])
    return exchange_sum(partial)


def solution(mesh):
    return jax.shard_map(
        functools.partial(on_device, mesh.shape["mem"]),
        mesh=mesh,
        in_specs=(
            P("grp", "mem", None),
            P("grp", None, None, None),
            P("grp", None, None, None, None),
            P("mem", None),
            P(),
            P(),
            P(),
        ),
        out_specs=P(("grp", "mem"), None),
        check_vma=False,
    )
```

```python
import functools

import jax
import jax.numpy as jnp
from jax import lax
from jax.experimental import pallas as pl
from jax.experimental.pallas import tpu as pltpu
from jax.sharding import PartitionSpec as P

QH = 32
KVH = 4
SUFFIX = 256
MOST_BLK = 32
GROUP = 8
NEG = -1e30
MESH = pl.DeviceIdType.MESH


def path_table(request_ids, node_blocks, root_of, mid_of):
    nodes_all = node_blocks.shape[0]
    middles_all = root_of.shape[0]
    leaves = mid_of.shape[0]
    roots_all = nodes_all - middles_all - leaves
    firsts = jnp.cumsum(node_blocks) - node_blocks
    middles = jnp.sum(
        jnp.where(jnp.arange(leaves)[None, :] == request_ids[:, None], mid_of[None, :], 0), axis=1
    )
    root_ids = jnp.sum(
        jnp.where(jnp.arange(middles_all)[None, :] == middles[:, None], root_of[None, :], 0), axis=1
    )
    path_nodes = jnp.stack(
        [root_ids, roots_all + middles, roots_all + middles_all + request_ids], axis=1
    )
    picked = jnp.arange(nodes_all)[None, None, :] == path_nodes[:, :, None]
    starts = jnp.sum(jnp.where(picked, firsts[None, None, :], 0), axis=2)
    counts = jnp.sum(jnp.where(picked, node_blocks[None, None, :], 0), axis=2)
    ends = jnp.cumsum(counts, axis=1)
    begins = ends - counts
    slots = jnp.arange(3 * MOST_BLK)[None, :]
    which = (slots >= ends[:, 0:1]).astype(jnp.int32) + (slots >= ends[:, 1:2]).astype(jnp.int32)
    which = jnp.minimum(which, 2)
    pick = jnp.arange(3)[None, None, :] == which[:, :, None]
    start_of = jnp.sum(jnp.where(pick, starts[:, None, :], 0), axis=2)
    begin_of = jnp.sum(jnp.where(pick, begins[:, None, :], 0), axis=2)
    ids = start_of + slots - begin_of
    total = ends[:, 2]
    ids = jnp.where(slots < total[:, None], ids, 0)
    return ids.astype(jnp.int32), total.astype(jnp.int32)


def suffix_kernel(q_ref, ks_ref, vs_ref, m_ref, l_ref, acc_ref):
    hd = q_ref.shape[-1]
    contract = (((1,), (1,)), ((), ()))
    scores = lax.dot_general(q_ref[...], ks_ref[...], contract, preferred_element_type=jnp.float32)
    scores = scores * hd ** (-0.5)
    tok = lax.broadcasted_iota(jnp.int32, scores.shape, 0) % SUFFIX
    key = lax.broadcasted_iota(jnp.int32, scores.shape, 1)
    scores = jnp.where(key <= tok, scores, NEG)
    high = jnp.max(scores, axis=-1, keepdims=True)
    weights = jnp.exp(scores - high)
    m_ref[...] = high
    l_ref[...] = jnp.sum(weights, axis=-1, keepdims=True)
    acc_ref[...] = jnp.dot(weights.astype(jnp.bfloat16), vs_ref[...], preferred_element_type=jnp.float32)


def suffix_attend(q, ks, vs):
    req, rows, hd = q.shape
    index = lambda j: (j, 0, 0)
    return pl.pallas_call(
        suffix_kernel,
        out_shape=(
            jax.ShapeDtypeStruct((req, rows, 1), jnp.float32),
            jax.ShapeDtypeStruct((req, rows, 1), jnp.float32),
            jax.ShapeDtypeStruct((req, rows, hd), jnp.float32),
        ),
        grid=(req,),
        in_specs=[
            pl.BlockSpec((None, rows, hd), index),
            pl.BlockSpec((None, SUFFIX, hd), index),
            pl.BlockSpec((None, SUFFIX, hd), index),
        ],
        out_specs=[
            pl.BlockSpec((None, rows, 1), index),
            pl.BlockSpec((None, rows, 1), index),
            pl.BlockSpec((None, rows, hd), index),
        ],
        compiler_params=pltpu.CompilerParams(dimension_semantics=("arbitrary",)),
    )(q, ks, vs)


def attend_kernel(slots, ids_ref, cnt_ref, q_ref, m0_ref, l0_ref, acc0_ref, kv_hbm, o_ref, kbuf, vbuf, sem, m_sc, l_sc, acc_sc):
    j = pl.program_id(0)
    n = cnt_ref[j]
    rows, hd = q_ref.shape
    scale = hd ** (-0.5)
    contract = (((1,), (1,)), ((), ()))
    q = q_ref[...]
    m_sc[...] = m0_ref[...]
    l_sc[...] = l0_ref[...]
    acc_sc[...] = acc0_ref[...]

    rows_blk = kbuf.shape[1] // GROUP
    steps = (n + GROUP - 1) // GROUP

    def copies(step, slot, fresh):
        for g in range(GROUP):
            bid = ids_ref[j * slots + step * GROUP + g] if fresh else 0
            for half, dst in ((0, kbuf), (1, vbuf)):
                yield pltpu.make_async_copy(
                    kv_hbm.at[bid, half],
                    dst.at[slot, pl.ds(g * rows_blk, rows_blk)],
                    sem.at[slot, g, half],
                )

    def fetch(step, slot):
        for c in copies(step, slot, True):
            c.start()

    @pl.when(steps > 0)
    def _():
        fetch(0, 0)

    def body(st, carry):
        slot = st % 2
        for c in copies(st, slot, False):
            c.wait()

        @pl.when(st + 1 < steps)
        def _():
            fetch(st + 1, 1 - slot)

        limit = (n - st * GROUP) * rows_blk

        def update(masked):
            s = lax.dot_general(q, kbuf[slot], contract, preferred_element_type=jnp.float32) * scale
            if masked:
                col = lax.broadcasted_iota(jnp.int32, s.shape, 1)
                s = jnp.where(col < limit, s, NEG)
            m_old = m_sc[...]
            m_new = jnp.maximum(m_old, jnp.max(s, axis=-1, keepdims=True))
            factor = jnp.exp(m_old - m_new)
            p = jnp.exp(s - m_new)
            l_sc[...] = l_sc[...] * factor + jnp.sum(p, axis=-1, keepdims=True)
            acc_sc[...] = acc_sc[...] * factor + jnp.dot(
                p.astype(jnp.bfloat16), vbuf[slot], preferred_element_type=jnp.float32
            )
            m_sc[...] = m_new

        @pl.when(limit >= kbuf.shape[1])
        def _():
            update(False)

        @pl.when(limit < kbuf.shape[1])
        def _():
            update(True)

        return carry

    lax.fori_loop(0, steps, body, 0)
    o_ref[...] = (acc_sc[...] / l_sc[...]).astype(o_ref.dtype)


def attend(ids, counts, q, state, kv_all):
    req, rows, hd = q.shape
    slots = ids.shape[1]
    block_shape = kv_all.shape[1:]
    return pl.pallas_call(
        functools.partial(attend_kernel, slots),
        out_shape=jax.ShapeDtypeStruct((req, rows, hd), jnp.bfloat16),
        grid_spec=pltpu.PrefetchScalarGridSpec(
            num_scalar_prefetch=2,
            grid=(req,),
            in_specs=[
                pl.BlockSpec((None, rows, hd), lambda j, ids, cnt: (j, 0, 0)),
                pl.BlockSpec((None, rows, 1), lambda j, ids, cnt: (j, 0, 0)),
                pl.BlockSpec((None, rows, 1), lambda j, ids, cnt: (j, 0, 0)),
                pl.BlockSpec((None, rows, hd), lambda j, ids, cnt: (j, 0, 0)),
                pl.BlockSpec(memory_space=pl.ANY),
            ],
            out_specs=pl.BlockSpec((None, rows, hd), lambda j, ids, cnt: (j, 0, 0)),
            scratch_shapes=[
                pltpu.VMEM((2, GROUP * block_shape[1], block_shape[2]), kv_all.dtype),
                pltpu.VMEM((2, GROUP * block_shape[1], block_shape[2]), kv_all.dtype),
                pltpu.SemaphoreType.DMA((2, GROUP, 2)),
                pltpu.VMEM((rows, 1), jnp.float32),
                pltpu.VMEM((rows, 1), jnp.float32),
                pltpu.VMEM((rows, hd), jnp.float32),
            ],
        ),
        compiler_params=pltpu.CompilerParams(dimension_semantics=("arbitrary",)),
    )(ids.reshape(-1), counts, q, *state, kv_all)


def exchange_kernel(n, a_ref, w_ref, o_ref, send, recv, send_sem, recv_sem):
    me = lax.axis_index("mem")
    grp = lax.axis_index("grp")
    heads, hd, cols = w_ref.shape
    rows = o_ref.shape[0]
    per_req = a_ref.shape[1] // heads // rows
    barrier = pltpu.get_barrier_semaphore()
    for k in range(1, n):
        pl.semaphore_signal(barrier, inc=1, device_id=(grp, lax.rem(me + k, n)), device_id_type=MESH)
    pl.semaphore_wait(barrier, n - 1)

    def chunk(peer):
        req = peer // per_req
        first = pl.multiple_of((peer % per_req) * rows, rows)
        total = jnp.zeros((rows, cols), jnp.float32)
        for h in range(heads):
            piece = a_ref[req, pl.ds(h * per_req * rows + first, rows), :]
            total = total + jnp.dot(piece, w_ref[h], preferred_element_type=jnp.float32)
        return total.astype(o_ref.dtype)

    copies = []
    for k in range(1, n):
        peer = lax.rem(me + k, n)
        send[k] = chunk(peer)
        copy = pltpu.make_async_remote_copy(
            src_ref=send.at[k],
            dst_ref=recv.at[k],
            send_sem=send_sem.at[k],
            recv_sem=recv_sem.at[k],
            device_id=(grp, peer),
            device_id_type=MESH,
        )
        copy.start()
        copies.append(copy)
    total = chunk(me).astype(jnp.float32)
    for k in range(1, n):
        copies[k - 1].wait()
        total = total + recv[k].astype(jnp.float32)
    o_ref[...] = total.astype(o_ref.dtype)


def exchange_sum(n, attended, w):
    heads, hd, cols = w.shape
    rows = attended.shape[0] * attended.shape[1] // heads // n
    return pl.pallas_call(
        functools.partial(exchange_kernel, n),
        out_shape=jax.ShapeDtypeStruct((rows, cols), jnp.bfloat16),
        in_specs=[pl.BlockSpec(memory_space=pltpu.VMEM)] * 2,
        out_specs=pl.BlockSpec(memory_space=pltpu.VMEM),
        scratch_shapes=[
            pltpu.VMEM((n, rows, cols), jnp.bfloat16),
            pltpu.VMEM((n, rows, cols), jnp.bfloat16),
            pltpu.SemaphoreType.DMA((n,)),
            pltpu.SemaphoreType.DMA((n,)),
        ],
        compiler_params=pltpu.CompilerParams(collective_id=0, has_side_effects=True),
    )(attended, w)


def on_device(n_mem, queries, suffix_kv, prefix_kv, out_weight, node_blocks, root_of, mid_of):
    group_index = lax.axis_index("grp")
    head_index = lax.axis_index("mem")
    tokens_dev, heads_dev, head_dim = queries.shape
    req_local = tokens_dev // SUFFIX
    group_size = QH // KVH
    kv_start = head_index * heads_dev // group_size
    prefix_part = lax.dynamic_index_in_dim(prefix_kv, kv_start, 3, keepdims=False)
    suffix_part = lax.dynamic_index_in_dim(suffix_kv, kv_start, 2, keepdims=False)
    kv_all = lax.all_gather(prefix_part, "grp", axis=0, tiled=True)

    request_ids = group_index * req_local + jnp.arange(req_local)
    ids, counts = path_table(request_ids, node_blocks, root_of, mid_of)

    q = queries.reshape(req_local, SUFFIX, heads_dev, head_dim).transpose(0, 2, 1, 3)
    q = q.reshape(req_local, heads_dev * SUFFIX, head_dim)
    ks = suffix_part[:, 0].reshape(req_local, SUFFIX, head_dim)
    vs = suffix_part[:, 1].reshape(req_local, SUFFIX, head_dim)
    attended = attend(ids, counts, q, suffix_attend(q, ks, vs), kv_all)
    w = out_weight.reshape(heads_dev, head_dim, out_weight.shape[1])
    return exchange_sum(n_mem, attended, w)


def solution(mesh):
    return jax.shard_map(
        functools.partial(on_device, mesh.shape["mem"]),
        mesh=mesh,
        in_specs=(
            P("grp", "mem", None),
            P("grp", None, None, None),
            P("grp", None, None, None, None),
            P("mem", None),
            P(),
            P(),
            P(),
        ),
        out_specs=P(("grp", "mem"), None),
        check_vma=False,
    )
```

```python
import functools

import jax
import jax.numpy as jnp
from jax import lax
from jax.experimental import pallas as pl
from jax.experimental.pallas import tpu as pltpu
from jax.sharding import PartitionSpec as P

QH = 32
KVH = 4
SUFFIX = 256
MOST_BLK = 32
GROUP = 8
NEG = -1e30
MESH = pl.DeviceIdType.MESH


def path_table(request_ids, node_blocks, root_of, mid_of):
    nodes_all = node_blocks.shape[0]
    middles_all = root_of.shape[0]
    leaves = mid_of.shape[0]
    roots_all = nodes_all - middles_all - leaves
    firsts = jnp.cumsum(node_blocks) - node_blocks
    middles = jnp.sum(
        jnp.where(jnp.arange(leaves)[None, :] == request_ids[:, None], mid_of[None, :], 0), axis=1
    )
    root_ids = jnp.sum(
        jnp.where(jnp.arange(middles_all)[None, :] == middles[:, None], root_of[None, :], 0), axis=1
    )
    path_nodes = jnp.stack(
        [root_ids, roots_all + middles, roots_all + middles_all + request_ids], axis=1
    )
    picked = jnp.arange(nodes_all)[None, None, :] == path_nodes[:, :, None]
    starts = jnp.sum(jnp.where(picked, firsts[None, None, :], 0), axis=2)
    counts = jnp.sum(jnp.where(picked, node_blocks[None, None, :], 0), axis=2)
    ends = jnp.cumsum(counts, axis=1)
    begins = ends - counts
    slots = jnp.arange(3 * MOST_BLK)[None, :]
    which = (slots >= ends[:, 0:1]).astype(jnp.int32) + (slots >= ends[:, 1:2]).astype(jnp.int32)
    which = jnp.minimum(which, 2)
    pick = jnp.arange(3)[None, None, :] == which[:, :, None]
    start_of = jnp.sum(jnp.where(pick, starts[:, None, :], 0), axis=2)
    begin_of = jnp.sum(jnp.where(pick, begins[:, None, :], 0), axis=2)
    ids = start_of + slots - begin_of
    total = ends[:, 2]
    ids = jnp.where(slots < total[:, None], ids, 0)
    return ids.astype(jnp.int32), total.astype(jnp.int32)


def suffix_kernel(q_ref, ks_ref, vs_ref, m_ref, l_ref, acc_ref):
    hd = q_ref.shape[-1]
    contract = (((1,), (1,)), ((), ()))
    scores = lax.dot_general(q_ref[...], ks_ref[...], contract, preferred_element_type=jnp.float32)
    scores = scores * hd ** (-0.5)
    tok = lax.broadcasted_iota(jnp.int32, scores.shape, 0) % SUFFIX
    key = lax.broadcasted_iota(jnp.int32, scores.shape, 1)
    scores = jnp.where(key <= tok, scores, NEG)
    high = jnp.max(scores, axis=-1, keepdims=True)
    weights = jnp.exp(scores - high)
    m_ref[...] = high
    l_ref[...] = jnp.sum(weights, axis=-1, keepdims=True)
    acc_ref[...] = jnp.dot(weights.astype(jnp.bfloat16), vs_ref[...], preferred_element_type=jnp.float32)


def suffix_attend(q, ks, vs):
    req, rows, hd = q.shape
    index = lambda j: (j, 0, 0)
    return pl.pallas_call(
        suffix_kernel,
        out_shape=(
            jax.ShapeDtypeStruct((req, rows, 1), jnp.float32),
            jax.ShapeDtypeStruct((req, rows, 1), jnp.float32),
            jax.ShapeDtypeStruct((req, rows, hd), jnp.float32),
        ),
        grid=(req,),
        in_specs=[
            pl.BlockSpec((None, rows, hd), index),
            pl.BlockSpec((None, SUFFIX, hd), index),
            pl.BlockSpec((None, SUFFIX, hd), index),
        ],
        out_specs=[
            pl.BlockSpec((None, rows, 1), index),
            pl.BlockSpec((None, rows, 1), index),
            pl.BlockSpec((None, rows, hd), index),
        ],
        compiler_params=pltpu.CompilerParams(dimension_semantics=("arbitrary",)),
    )(q, ks, vs)


def attend_kernel(slots, ids_ref, cnt_ref, q_ref, m0_ref, l0_ref, acc0_ref, kv_hbm, o_ref, kbuf, vbuf, sem, m_sc, l_sc, acc_sc):
    j = pl.program_id(0)
    n = cnt_ref[j]
    rows, hd = q_ref.shape
    scale = hd ** (-0.5)
    contract = (((1,), (1,)), ((), ()))
    q = q_ref[...]
    m_sc[...] = m0_ref[...]
    l_sc[...] = l0_ref[...]
    acc_sc[...] = acc0_ref[...]

    rows_blk = kbuf.shape[1] // GROUP
    steps = (n + GROUP - 1) // GROUP

    def copies(step, slot, fresh):
        for g in range(GROUP):
            bid = ids_ref[j * slots + step * GROUP + g] if fresh else 0
            for half, dst in ((0, kbuf), (1, vbuf)):
                yield pltpu.make_async_copy(
                    kv_hbm.at[bid, half],
                    dst.at[slot, pl.ds(g * rows_blk, rows_blk)],
                    sem.at[slot, g, half],
                )

    def fetch(step, slot):
        for c in copies(step, slot, True):
            c.start()

    @pl.when(steps > 0)
    def _():
        fetch(0, 0)

    def body(st, carry):
        slot = st % 2
        for c in copies(st, slot, False):
            c.wait()

        @pl.when(st + 1 < steps)
        def _():
            fetch(st + 1, 1 - slot)

        limit = (n - st * GROUP) * rows_blk

        def update(masked):
            s = lax.dot_general(q, kbuf[slot], contract, preferred_element_type=jnp.float32) * scale
            if masked:
                col = lax.broadcasted_iota(jnp.int32, s.shape, 1)
                s = jnp.where(col < limit, s, NEG)
            m_old = m_sc[...]
            m_new = jnp.maximum(m_old, jnp.max(s, axis=-1, keepdims=True))
            factor = jnp.exp(m_old - m_new)
            p = jnp.exp(s - m_new)
            l_sc[...] = l_sc[...] * factor + jnp.sum(p, axis=-1, keepdims=True)
            acc_sc[...] = acc_sc[...] * factor + jnp.dot(
                p.astype(jnp.bfloat16), vbuf[slot], preferred_element_type=jnp.float32
            )
            m_sc[...] = m_new

        @pl.when(limit >= kbuf.shape[1])
        def _():
            update(False)

        @pl.when(limit < kbuf.shape[1])
        def _():
            update(True)

        return carry

    lax.fori_loop(0, steps, body, 0)
    o_ref[...] = (acc_sc[...] / l_sc[...]).astype(o_ref.dtype)


def attend(ids, counts, q, state, kv_all):
    req, rows, hd = q.shape
    slots = ids.shape[1]
    block_shape = kv_all.shape[1:]
    return pl.pallas_call(
        functools.partial(attend_kernel, slots),
        out_shape=jax.ShapeDtypeStruct((req, rows, hd), jnp.bfloat16),
        grid_spec=pltpu.PrefetchScalarGridSpec(
            num_scalar_prefetch=2,
            grid=(req,),
            in_specs=[
                pl.BlockSpec((None, rows, hd), lambda j, ids, cnt: (j, 0, 0)),
                pl.BlockSpec((None, rows, 1), lambda j, ids, cnt: (j, 0, 0)),
                pl.BlockSpec((None, rows, 1), lambda j, ids, cnt: (j, 0, 0)),
                pl.BlockSpec((None, rows, hd), lambda j, ids, cnt: (j, 0, 0)),
                pl.BlockSpec(memory_space=pl.ANY),
            ],
            out_specs=pl.BlockSpec((None, rows, hd), lambda j, ids, cnt: (j, 0, 0)),
            scratch_shapes=[
                pltpu.VMEM((2, GROUP * block_shape[1], block_shape[2]), kv_all.dtype),
                pltpu.VMEM((2, GROUP * block_shape[1], block_shape[2]), kv_all.dtype),
                pltpu.SemaphoreType.DMA((2, GROUP, 2)),
                pltpu.VMEM((rows, 1), jnp.float32),
                pltpu.VMEM((rows, 1), jnp.float32),
                pltpu.VMEM((rows, hd), jnp.float32),
            ],
        ),
        compiler_params=pltpu.CompilerParams(dimension_semantics=("arbitrary",)),
    )(ids.reshape(-1), counts, q, *state, kv_all)


def exchange_kernel(n, a_ref, w_ref, o_ref, send, recv, send_sem, recv_sem):
    me = lax.axis_index("mem")
    grp = lax.axis_index("grp")
    heads, hd, cols = w_ref.shape
    rows = o_ref.shape[0]
    per_req = a_ref.shape[1] // heads // rows
    barrier = pltpu.get_barrier_semaphore()
    for k in range(1, n):
        pl.semaphore_signal(barrier, inc=1, device_id=(grp, lax.rem(me + k, n)), device_id_type=MESH)
    pl.semaphore_wait(barrier, n - 1)

    def chunk(peer):
        req = peer // per_req
        first = pl.multiple_of((peer % per_req) * rows, rows)
        total = jnp.zeros((rows, cols), jnp.float32)
        for h in range(heads):
            piece = a_ref[req, pl.ds(h * per_req * rows + first, rows), :]
            total = total + jnp.dot(piece, w_ref[h], preferred_element_type=jnp.float32)
        return total.astype(o_ref.dtype)

    copies = []
    for k in range(1, n):
        peer = lax.rem(me + k, n)
        send[k] = chunk(peer)
        copy = pltpu.make_async_remote_copy(
            src_ref=send.at[k],
            dst_ref=recv.at[k],
            send_sem=send_sem.at[k],
            recv_sem=recv_sem.at[k],
            device_id=(grp, peer),
            device_id_type=MESH,
        )
        copy.start()
        copies.append(copy)
    total = chunk(me).astype(jnp.float32)
    for k in range(1, n):
        copies[k - 1].wait()
        total = total + recv[k].astype(jnp.float32)
    o_ref[...] = total.astype(o_ref.dtype)


def exchange_sum(n, attended, w):
    heads, hd, cols = w.shape
    rows = attended.shape[0] * attended.shape[1] // heads // n
    return pl.pallas_call(
        functools.partial(exchange_kernel, n),
        out_shape=jax.ShapeDtypeStruct((rows, cols), jnp.bfloat16),
        in_specs=[pl.BlockSpec(memory_space=pltpu.VMEM)] * 2,
        out_specs=pl.BlockSpec(memory_space=pltpu.VMEM),
        scratch_shapes=[
            pltpu.VMEM((n, rows, cols), jnp.bfloat16),
            pltpu.VMEM((n, rows, cols), jnp.bfloat16),
            pltpu.SemaphoreType.DMA((n,)),
            pltpu.SemaphoreType.DMA((n,)),
        ],
        compiler_params=pltpu.CompilerParams(collective_id=0, has_side_effects=True),
    )(attended, w)


def on_device(n_mem, queries, suffix_kv, prefix_kv, out_weight, node_blocks, root_of, mid_of):
    group_index = lax.axis_index("grp")
    head_index = lax.axis_index("mem")
    tokens_dev, heads_dev, head_dim = queries.shape
    req_local = tokens_dev // SUFFIX
    group_size = QH // KVH
    kv_start = head_index * heads_dev // group_size
    heads_kv = jnp.arange(prefix_kv.shape[3])[None, None, None, :, None]
    prefix_part = jnp.sum(jnp.where(heads_kv == kv_start, prefix_kv, jnp.zeros_like(prefix_kv)), axis=3)
    suffix_part = lax.dynamic_index_in_dim(suffix_kv, kv_start, 2, keepdims=False)
    kv_all = lax.all_gather(prefix_part, "grp", axis=0, tiled=True)

    request_ids = group_index * req_local + jnp.arange(req_local)
    ids, counts = path_table(request_ids, node_blocks, root_of, mid_of)

    q = queries.reshape(req_local, SUFFIX, heads_dev, head_dim).transpose(0, 2, 1, 3)
    q = q.reshape(req_local, heads_dev * SUFFIX, head_dim)
    ks = suffix_part[:, 0].reshape(req_local, SUFFIX, head_dim)
    vs = suffix_part[:, 1].reshape(req_local, SUFFIX, head_dim)
    attended = attend(ids, counts, q, suffix_attend(q, ks, vs), kv_all)
    w = out_weight.reshape(heads_dev, head_dim, out_weight.shape[1])
    return exchange_sum(n_mem, attended, w)


def solution(mesh):
    return jax.shard_map(
        functools.partial(on_device, mesh.shape["mem"]),
        mesh=mesh,
        in_specs=(
            P("grp", "mem", None),
            P("grp", None, None, None),
            P("grp", None, None, None, None),
            P("mem", None),
            P(),
            P(),
            P(),
        ),
        out_specs=P(("grp", "mem"), None),
        check_vma=False,
    )
```

```python
import functools

import jax
import jax.numpy as jnp
from jax import lax
from jax.experimental import pallas as pl
from jax.experimental.pallas import tpu as pltpu
from jax.sharding import PartitionSpec as P

QH = 32
KVH = 4
SUFFIX = 256
MOST_BLK = 32
GROUP = 16
NEG = -1e30
MESH = pl.DeviceIdType.MESH


def path_table(request_ids, node_blocks, root_of, mid_of):
    nodes_all = node_blocks.shape[0]
    middles_all = root_of.shape[0]
    leaves = mid_of.shape[0]
    roots_all = nodes_all - middles_all - leaves
    firsts = jnp.cumsum(node_blocks) - node_blocks
    middles = jnp.sum(
        jnp.where(jnp.arange(leaves)[None, :] == request_ids[:, None], mid_of[None, :], 0), axis=1
    )
    root_ids = jnp.sum(
        jnp.where(jnp.arange(middles_all)[None, :] == middles[:, None], root_of[None, :], 0), axis=1
    )
    path_nodes = jnp.stack(
        [root_ids, roots_all + middles, roots_all + middles_all + request_ids], axis=1
    )
    picked = jnp.arange(nodes_all)[None, None, :] == path_nodes[:, :, None]
    starts = jnp.sum(jnp.where(picked, firsts[None, None, :], 0), axis=2)
    counts = jnp.sum(jnp.where(picked, node_blocks[None, None, :], 0), axis=2)
    ends = jnp.cumsum(counts, axis=1)
    begins = ends - counts
    slots = jnp.arange(3 * MOST_BLK)[None, :]
    which = (slots >= ends[:, 0:1]).astype(jnp.int32) + (slots >= ends[:, 1:2]).astype(jnp.int32)
    which = jnp.minimum(which, 2)
    pick = jnp.arange(3)[None, None, :] == which[:, :, None]
    start_of = jnp.sum(jnp.where(pick, starts[:, None, :], 0), axis=2)
    begin_of = jnp.sum(jnp.where(pick, begins[:, None, :], 0), axis=2)
    ids = start_of + slots - begin_of
    total = ends[:, 2]
    ids = jnp.where(slots < total[:, None], ids, 0)
    return ids.astype(jnp.int32), total.astype(jnp.int32)


def suffix_kernel(q_ref, ks_ref, vs_ref, m_ref, l_ref, acc_ref):
    hd = q_ref.shape[-1]
    contract = (((1,), (1,)), ((), ()))
    scores = lax.dot_general(q_ref[...], ks_ref[...], contract, preferred_element_type=jnp.float32)
    scores = scores * hd ** (-0.5)
    tok = lax.broadcasted_iota(jnp.int32, scores.shape, 0) % SUFFIX
    key = lax.broadcasted_iota(jnp.int32, scores.shape, 1)
    scores = jnp.where(key <= tok, scores, NEG)
    high = jnp.max(scores, axis=-1, keepdims=True)
    weights = jnp.exp(scores - high)
    m_ref[...] = high
    l_ref[...] = jnp.sum(weights, axis=-1, keepdims=True)
    acc_ref[...] = jnp.dot(weights.astype(jnp.bfloat16), vs_ref[...], preferred_element_type=jnp.float32)


def suffix_attend(q, ks, vs):
    req, rows, hd = q.shape
    index = lambda j: (j, 0, 0)
    return pl.pallas_call(
        suffix_kernel,
        out_shape=(
            jax.ShapeDtypeStruct((req, rows, 1), jnp.float32),
            jax.ShapeDtypeStruct((req, rows, 1), jnp.float32),
            jax.ShapeDtypeStruct((req, rows, hd), jnp.float32),
        ),
        grid=(req,),
        in_specs=[
            pl.BlockSpec((None, rows, hd), index),
            pl.BlockSpec((None, SUFFIX, hd), index),
            pl.BlockSpec((None, SUFFIX, hd), index),
        ],
        out_specs=[
            pl.BlockSpec((None, rows, 1), index),
            pl.BlockSpec((None, rows, 1), index),
            pl.BlockSpec((None, rows, hd), index),
        ],
        compiler_params=pltpu.CompilerParams(dimension_semantics=("arbitrary",)),
    )(q, ks, vs)


def attend_kernel(slots, ids_ref, cnt_ref, q_ref, m0_ref, l0_ref, acc0_ref, kv_hbm, o_ref, kbuf, vbuf, sem, m_sc, l_sc, acc_sc):
    j = pl.program_id(0)
    n = cnt_ref[j]
    rows, hd = q_ref.shape
    scale = hd ** (-0.5)
    contract = (((1,), (1,)), ((), ()))
    q = q_ref[...]
    m_sc[...] = m0_ref[...]
    l_sc[...] = l0_ref[...]
    acc_sc[...] = acc0_ref[...]

    rows_blk = kbuf.shape[1] // GROUP
    steps = (n + GROUP - 1) // GROUP

    def copies(step, slot, fresh):
        for g in range(GROUP):
            bid = ids_ref[j * slots + step * GROUP + g] if fresh else 0
            for half, dst in ((0, kbuf), (1, vbuf)):
                yield pltpu.make_async_copy(
                    kv_hbm.at[bid, half],
                    dst.at[slot, pl.ds(g * rows_blk, rows_blk)],
                    sem.at[slot, g, half],
                )

    def fetch(step, slot):
        for c in copies(step, slot, True):
            c.start()

    @pl.when(steps > 0)
    def _():
        fetch(0, 0)

    def body(st, carry):
        slot = st % 2
        for c in copies(st, slot, False):
            c.wait()

        @pl.when(st + 1 < steps)
        def _():
            fetch(st + 1, 1 - slot)

        limit = (n - st * GROUP) * rows_blk

        def update(masked):
            s = lax.dot_general(q, kbuf[slot], contract, preferred_element_type=jnp.float32) * scale
            if masked:
                col = lax.broadcasted_iota(jnp.int32, s.shape, 1)
                s = jnp.where(col < limit, s, NEG)
            m_old = m_sc[...]
            m_new = jnp.maximum(m_old, jnp.max(s, axis=-1, keepdims=True))
            factor = jnp.exp(m_old - m_new)
            p = jnp.exp(s - m_new)
            l_sc[...] = l_sc[...] * factor + jnp.sum(p, axis=-1, keepdims=True)
            acc_sc[...] = acc_sc[...] * factor + jnp.dot(
                p.astype(jnp.bfloat16), vbuf[slot], preferred_element_type=jnp.float32
            )
            m_sc[...] = m_new

        @pl.when(limit >= kbuf.shape[1])
        def _():
            update(False)

        @pl.when(limit < kbuf.shape[1])
        def _():
            update(True)

        return carry

    lax.fori_loop(0, steps, body, 0)
    o_ref[...] = (acc_sc[...] / l_sc[...]).astype(o_ref.dtype)


def attend(ids, counts, q, state, kv_all):
    req, rows, hd = q.shape
    slots = ids.shape[1]
    block_shape = kv_all.shape[1:]
    return pl.pallas_call(
        functools.partial(attend_kernel, slots),
        out_shape=jax.ShapeDtypeStruct((req, rows, hd), jnp.bfloat16),
        grid_spec=pltpu.PrefetchScalarGridSpec(
            num_scalar_prefetch=2,
            grid=(req,),
            in_specs=[
                pl.BlockSpec((None, rows, hd), lambda j, ids, cnt: (j, 0, 0)),
                pl.BlockSpec((None, rows, 1), lambda j, ids, cnt: (j, 0, 0)),
                pl.BlockSpec((None, rows, 1), lambda j, ids, cnt: (j, 0, 0)),
                pl.BlockSpec((None, rows, hd), lambda j, ids, cnt: (j, 0, 0)),
                pl.BlockSpec(memory_space=pl.ANY),
            ],
            out_specs=pl.BlockSpec((None, rows, hd), lambda j, ids, cnt: (j, 0, 0)),
            scratch_shapes=[
                pltpu.VMEM((2, GROUP * block_shape[1], block_shape[2]), kv_all.dtype),
                pltpu.VMEM((2, GROUP * block_shape[1], block_shape[2]), kv_all.dtype),
                pltpu.SemaphoreType.DMA((2, GROUP, 2)),
                pltpu.VMEM((rows, 1), jnp.float32),
                pltpu.VMEM((rows, 1), jnp.float32),
                pltpu.VMEM((rows, hd), jnp.float32),
            ],
        ),
        compiler_params=pltpu.CompilerParams(dimension_semantics=("arbitrary",)),
    )(ids.reshape(-1), counts, q, *state, kv_all)


def exchange_kernel(n, a_ref, w_ref, o_ref, send, recv, send_sem, recv_sem):
    me = lax.axis_index("mem")
    grp = lax.axis_index("grp")
    heads, hd, cols = w_ref.shape
    rows = o_ref.shape[0]
    per_req = a_ref.shape[1] // heads // rows
    barrier = pltpu.get_barrier_semaphore()
    for k in range(1, n):
        pl.semaphore_signal(barrier, inc=1, device_id=(grp, lax.rem(me + k, n)), device_id_type=MESH)
    pl.semaphore_wait(barrier, n - 1)

    def chunk(peer):
        req = peer // per_req
        first = pl.multiple_of((peer % per_req) * rows, rows)
        total = jnp.zeros((rows, cols), jnp.float32)
        for h in range(heads):
            piece = a_ref[req, pl.ds(h * per_req * rows + first, rows), :]
            total = total + jnp.dot(piece, w_ref[h], preferred_element_type=jnp.float32)
        return total.astype(o_ref.dtype)

    copies = []
    for k in range(1, n):
        peer = lax.rem(me + k, n)
        send[k] = chunk(peer)
        copy = pltpu.make_async_remote_copy(
            src_ref=send.at[k],
            dst_ref=recv.at[k],
            send_sem=send_sem.at[k],
            recv_sem=recv_sem.at[k],
            device_id=(grp, peer),
            device_id_type=MESH,
        )
        copy.start()
        copies.append(copy)
    total = chunk(me).astype(jnp.float32)
    for k in range(1, n):
        copies[k - 1].wait()
        total = total + recv[k].astype(jnp.float32)
    o_ref[...] = total.astype(o_ref.dtype)


def exchange_sum(n, attended, w):
    heads, hd, cols = w.shape
    rows = attended.shape[0] * attended.shape[1] // heads // n
    return pl.pallas_call(
        functools.partial(exchange_kernel, n),
        out_shape=jax.ShapeDtypeStruct((rows, cols), jnp.bfloat16),
        in_specs=[pl.BlockSpec(memory_space=pltpu.VMEM)] * 2,
        out_specs=pl.BlockSpec(memory_space=pltpu.VMEM),
        scratch_shapes=[
            pltpu.VMEM((n, rows, cols), jnp.bfloat16),
            pltpu.VMEM((n, rows, cols), jnp.bfloat16),
            pltpu.SemaphoreType.DMA((n,)),
            pltpu.SemaphoreType.DMA((n,)),
        ],
        compiler_params=pltpu.CompilerParams(collective_id=0, has_side_effects=True),
    )(attended, w)


def on_device(n_mem, queries, suffix_kv, prefix_kv, out_weight, node_blocks, root_of, mid_of):
    group_index = lax.axis_index("grp")
    head_index = lax.axis_index("mem")
    tokens_dev, heads_dev, head_dim = queries.shape
    req_local = tokens_dev // SUFFIX
    group_size = QH // KVH
    kv_start = head_index * heads_dev // group_size
    prefix_part = lax.dynamic_index_in_dim(prefix_kv, kv_start, 3, keepdims=False)
    suffix_part = lax.dynamic_index_in_dim(suffix_kv, kv_start, 2, keepdims=False)
    kv_all = lax.all_gather(prefix_part, "grp", axis=0, tiled=True)

    request_ids = group_index * req_local + jnp.arange(req_local)
    ids, counts = path_table(request_ids, node_blocks, root_of, mid_of)

    q = queries.reshape(req_local, SUFFIX, heads_dev, head_dim).transpose(0, 2, 1, 3)
    q = q.reshape(req_local, heads_dev * SUFFIX, head_dim)
    ks = suffix_part[:, 0].reshape(req_local, SUFFIX, head_dim)
    vs = suffix_part[:, 1].reshape(req_local, SUFFIX, head_dim)
    attended = attend(ids, counts, q, suffix_attend(q, ks, vs), kv_all)
    w = out_weight.reshape(heads_dev, head_dim, out_weight.shape[1])
    return exchange_sum(n_mem, attended, w)


def solution(mesh):
    return jax.shard_map(
        functools.partial(on_device, mesh.shape["mem"]),
        mesh=mesh,
        in_specs=(
            P("grp", "mem", None),
            P("grp", None, None, None),
            P("grp", None, None, None, None),
            P("mem", None),
            P(),
            P(),
            P(),
        ),
        out_specs=P(("grp", "mem"), None),
        check_vma=False,
    )
```

```python
import functools

import jax
import jax.numpy as jnp
from jax import lax
from jax.experimental import pallas as pl
from jax.experimental.pallas import tpu as pltpu
from jax.sharding import PartitionSpec as P

QH = 32
KVH = 4
SUFFIX = 256
MOST_BLK = 32
GROUP = 8
NEG = -1e30
MESH = pl.DeviceIdType.MESH


def path_table(request_ids, node_blocks, root_of, mid_of):
    nodes_all = node_blocks.shape[0]
    middles_all = root_of.shape[0]
    leaves = mid_of.shape[0]
    roots_all = nodes_all - middles_all - leaves
    firsts = jnp.cumsum(node_blocks) - node_blocks
    middles = jnp.sum(
        jnp.where(jnp.arange(leaves)[None, :] == request_ids[:, None], mid_of[None, :], 0), axis=1
    )
    root_ids = jnp.sum(
        jnp.where(jnp.arange(middles_all)[None, :] == middles[:, None], root_of[None, :], 0), axis=1
    )
    path_nodes = jnp.stack(
        [root_ids, roots_all + middles, roots_all + middles_all + request_ids], axis=1
    )
    picked = jnp.arange(nodes_all)[None, None, :] == path_nodes[:, :, None]
    starts = jnp.sum(jnp.where(picked, firsts[None, None, :], 0), axis=2)
    counts = jnp.sum(jnp.where(picked, node_blocks[None, None, :], 0), axis=2)
    ends = jnp.cumsum(counts, axis=1)
    begins = ends - counts
    slots = jnp.arange(3 * MOST_BLK)[None, :]
    which = (slots >= ends[:, 0:1]).astype(jnp.int32) + (slots >= ends[:, 1:2]).astype(jnp.int32)
    which = jnp.minimum(which, 2)
    pick = jnp.arange(3)[None, None, :] == which[:, :, None]
    start_of = jnp.sum(jnp.where(pick, starts[:, None, :], 0), axis=2)
    begin_of = jnp.sum(jnp.where(pick, begins[:, None, :], 0), axis=2)
    ids = start_of + slots - begin_of
    total = ends[:, 2]
    ids = jnp.where(slots < total[:, None], ids, 0)
    return ids.astype(jnp.int32), total.astype(jnp.int32)


def suffix_kernel(q_ref, ks_ref, vs_ref, m_ref, l_ref, acc_ref):
    hd = q_ref.shape[-1]
    contract = (((1,), (1,)), ((), ()))
    scores = lax.dot_general(q_ref[...], ks_ref[...], contract, preferred_element_type=jnp.float32)
    scores = scores * hd ** (-0.5)
    tok = lax.broadcasted_iota(jnp.int32, scores.shape, 0) % SUFFIX
    key = lax.broadcasted_iota(jnp.int32, scores.shape, 1)
    scores = jnp.where(key <= tok, scores, NEG)
    high = jnp.max(scores, axis=-1, keepdims=True)
    weights = jnp.exp(scores - high)
    m_ref[...] = high
    l_ref[...] = jnp.sum(weights, axis=-1, keepdims=True)
    acc_ref[...] = jnp.dot(weights.astype(jnp.bfloat16), vs_ref[...], preferred_element_type=jnp.float32)


def suffix_attend(q, ks, vs):
    req, rows, hd = q.shape
    index = lambda j: (j, 0, 0)
    return pl.pallas_call(
        suffix_kernel,
        out_shape=(
            jax.ShapeDtypeStruct((req, rows, 1), jnp.float32),
            jax.ShapeDtypeStruct((req, rows, 1), jnp.float32),
            jax.ShapeDtypeStruct((req, rows, hd), jnp.float32),
        ),
        grid=(req,),
        in_specs=[
            pl.BlockSpec((None, rows, hd), index),
            pl.BlockSpec((None, SUFFIX, hd), index),
            pl.BlockSpec((None, SUFFIX, hd), index),
        ],
        out_specs=[
            pl.BlockSpec((None, rows, 1), index),
            pl.BlockSpec((None, rows, 1), index),
            pl.BlockSpec((None, rows, hd), index),
        ],
        compiler_params=pltpu.CompilerParams(dimension_semantics=("arbitrary",)),
    )(q, ks, vs)


def attend_kernel(slots, ids_ref, cnt_ref, q_ref, m0_ref, l0_ref, acc0_ref, kv_hbm, o_ref, kbuf, vbuf, sem, m_sc, l_sc, acc_sc):
    j = pl.program_id(0)
    n = cnt_ref[j]
    rows, hd = q_ref.shape
    scale = hd ** (-0.5)
    contract = (((1,), (1,)), ((), ()))
    q = q_ref[...]
    m_sc[...] = m0_ref[...]
    l_sc[...] = l0_ref[...]
    acc_sc[...] = acc0_ref[...]

    rows_blk = kbuf.shape[1] // GROUP
    steps = (n + GROUP - 1) // GROUP

    def copies(step, slot, fresh):
        for g in range(GROUP):
            bid = ids_ref[j * slots + step * GROUP + g] if fresh else 0
            for half, dst in ((0, kbuf), (1, vbuf)):
                yield pltpu.make_async_copy(
                    kv_hbm.at[bid, half],
                    dst.at[slot, pl.ds(g * rows_blk, rows_blk)],
                    sem.at[slot, g, half],
                )

    def fetch(step, slot):
        for c in copies(step, slot, True):
            c.start()

    @pl.when(steps > 0)
    def _():
        fetch(0, 0)

    def body(st, carry):
        slot = st % 2
        for c in copies(st, slot, False):
            c.wait()

        @pl.when(st + 1 < steps)
        def _():
            fetch(st + 1, 1 - slot)

        limit = (n - st * GROUP) * rows_blk

        def update(masked):
            s = lax.dot_general(q, kbuf[slot], contract, preferred_element_type=jnp.float32) * scale
            if masked:
                col = lax.broadcasted_iota(jnp.int32, s.shape, 1)
                s = jnp.where(col < limit, s, NEG)
            m_old = m_sc[...]
            m_new = jnp.maximum(m_old, jnp.max(s, axis=-1, keepdims=True))
            factor = jnp.exp(m_old - m_new)
            p = jnp.exp(s - m_new)
            l_sc[...] = l_sc[...] * factor + jnp.sum(p, axis=-1, keepdims=True)
            acc_sc[...] = acc_sc[...] * factor + jnp.dot(
                p.astype(jnp.bfloat16), vbuf[slot], preferred_element_type=jnp.float32
            )
            m_sc[...] = m_new

        @pl.when(limit >= kbuf.shape[1])
        def _():
            update(False)

        @pl.when(limit < kbuf.shape[1])
        def _():
            update(True)

        return carry

    lax.fori_loop(0, steps, body, 0)
    o_ref[...] = (acc_sc[...] / l_sc[...]).astype(o_ref.dtype)


def attend(ids, counts, q, state, kv_all):
    req, rows, hd = q.shape
    slots = ids.shape[1]
    block_shape = kv_all.shape[1:]
    return pl.pallas_call(
        functools.partial(attend_kernel, slots),
        out_shape=jax.ShapeDtypeStruct((req, rows, hd), jnp.bfloat16),
        grid_spec=pltpu.PrefetchScalarGridSpec(
            num_scalar_prefetch=2,
            grid=(req,),
            in_specs=[
                pl.BlockSpec((None, rows, hd), lambda j, ids, cnt: (j, 0, 0)),
                pl.BlockSpec((None, rows, 1), lambda j, ids, cnt: (j, 0, 0)),
                pl.BlockSpec((None, rows, 1), lambda j, ids, cnt: (j, 0, 0)),
                pl.BlockSpec((None, rows, hd), lambda j, ids, cnt: (j, 0, 0)),
                pl.BlockSpec(memory_space=pl.ANY),
            ],
            out_specs=pl.BlockSpec((None, rows, hd), lambda j, ids, cnt: (j, 0, 0)),
            scratch_shapes=[
                pltpu.VMEM((2, GROUP * block_shape[1], block_shape[2]), kv_all.dtype),
                pltpu.VMEM((2, GROUP * block_shape[1], block_shape[2]), kv_all.dtype),
                pltpu.SemaphoreType.DMA((2, GROUP, 2)),
                pltpu.VMEM((rows, 1), jnp.float32),
                pltpu.VMEM((rows, 1), jnp.float32),
                pltpu.VMEM((rows, hd), jnp.float32),
            ],
        ),
        compiler_params=pltpu.CompilerParams(dimension_semantics=("arbitrary",)),
    )(ids.reshape(-1), counts, q, *state, kv_all)


def exchange_kernel(n, a_ref, w_ref, o_ref, send, recv, send_sem, recv_sem):
    me = lax.axis_index("mem")
    grp = lax.axis_index("grp")
    heads, hd, cols = w_ref.shape
    rows = o_ref.shape[0]
    per_req = a_ref.shape[1] // heads // rows
    barrier = pltpu.get_barrier_semaphore()
    for k in range(1, n):
        pl.semaphore_signal(barrier, inc=1, device_id=(grp, lax.rem(me + k, n)), device_id_type=MESH)
    pl.semaphore_wait(barrier, n - 1)

    def chunk(peer):
        req = peer // per_req
        first = pl.multiple_of((peer % per_req) * rows, rows)
        total = jnp.zeros((rows, cols), jnp.float32)
        for h in range(heads):
            piece = a_ref[req, pl.ds(h * per_req * rows + first, rows), :]
            total = total + jnp.dot(piece, w_ref[h], preferred_element_type=jnp.float32)
        return total.astype(o_ref.dtype)

    n_y = n // 2
    x_hi, y = me // n_y, me % n_y
    shifts = [(a, b) for a in range(2) for b in range(n_y) if (a, b) != (0, 0)]
    shifts.sort(key=lambda ab: -(2 * ab[0] + min(ab[1], n_y - ab[1])))
    copies = []
    for a, b in shifts:
        k = a * n_y + b
        peer = ((x_hi + a) % 2) * n_y + (y + b) % n_y
        send[k] = chunk(peer)
        copy = pltpu.make_async_remote_copy(
            src_ref=send.at[k],
            dst_ref=recv.at[k],
            send_sem=send_sem.at[k],
            recv_sem=recv_sem.at[k],
            device_id=(grp, peer),
            device_id_type=MESH,
        )
        copy.start()
        copies.append((k, copy))
    total = chunk(me).astype(jnp.float32)
    for k, copy in copies:
        copy.wait()
        total = total + recv[k].astype(jnp.float32)
    o_ref[...] = total.astype(o_ref.dtype)


def exchange_sum(n, attended, w):
    heads, hd, cols = w.shape
    rows = attended.shape[0] * attended.shape[1] // heads // n
    return pl.pallas_call(
        functools.partial(exchange_kernel, n),
        out_shape=jax.ShapeDtypeStruct((rows, cols), jnp.bfloat16),
        in_specs=[pl.BlockSpec(memory_space=pltpu.VMEM)] * 2,
        out_specs=pl.BlockSpec(memory_space=pltpu.VMEM),
        scratch_shapes=[
            pltpu.VMEM((n, rows, cols), jnp.bfloat16),
            pltpu.VMEM((n, rows, cols), jnp.bfloat16),
            pltpu.SemaphoreType.DMA((n,)),
            pltpu.SemaphoreType.DMA((n,)),
        ],
        compiler_params=pltpu.CompilerParams(collective_id=0, has_side_effects=True),
    )(attended, w)


def on_device(n_mem, queries, suffix_kv, prefix_kv, out_weight, node_blocks, root_of, mid_of):
    group_index = lax.axis_index("grp")
    head_index = lax.axis_index("mem")
    tokens_dev, heads_dev, head_dim = queries.shape
    req_local = tokens_dev // SUFFIX
    group_size = QH // KVH
    kv_start = head_index * heads_dev // group_size
    prefix_part = lax.dynamic_index_in_dim(prefix_kv, kv_start, 3, keepdims=False)
    suffix_part = lax.dynamic_index_in_dim(suffix_kv, kv_start, 2, keepdims=False)
    kv_all = lax.all_gather(prefix_part, "grp", axis=0, tiled=True)

    request_ids = group_index * req_local + jnp.arange(req_local)
    ids, counts = path_table(request_ids, node_blocks, root_of, mid_of)

    q = queries.reshape(req_local, SUFFIX, heads_dev, head_dim).transpose(0, 2, 1, 3)
    q = q.reshape(req_local, heads_dev * SUFFIX, head_dim)
    ks = suffix_part[:, 0].reshape(req_local, SUFFIX, head_dim)
    vs = suffix_part[:, 1].reshape(req_local, SUFFIX, head_dim)
    attended = attend(ids, counts, q, suffix_attend(q, ks, vs), kv_all)
    w = out_weight.reshape(heads_dev, head_dim, out_weight.shape[1])
    return exchange_sum(n_mem, attended, w)


def solution(mesh):
    return jax.shard_map(
        functools.partial(on_device, mesh.shape["mem"]),
        mesh=mesh,
        in_specs=(
            P("grp", "mem", None),
            P("grp", None, None, None),
            P("grp", None, None, None, None),
            P("mem", None),
            P(),
            P(),
            P(),
        ),
        out_specs=P(("grp", "mem"), None),
        check_vma=False,
    )
```

```python
import functools

import jax
import jax.numpy as jnp
from jax import lax
from jax.experimental import pallas as pl
from jax.experimental.pallas import tpu as pltpu
from jax.sharding import PartitionSpec as P

QH = 32
KVH = 4
SUFFIX = 256
MOST_BLK = 32
GROUP = 8
NEG = -1e30
MESH = pl.DeviceIdType.MESH


def path_table(request_ids, node_blocks, root_of, mid_of):
    nodes_all = node_blocks.shape[0]
    middles_all = root_of.shape[0]
    leaves = mid_of.shape[0]
    roots_all = nodes_all - middles_all - leaves
    firsts = jnp.cumsum(node_blocks) - node_blocks
    middles = jnp.sum(
        jnp.where(jnp.arange(leaves)[None, :] == request_ids[:, None], mid_of[None, :], 0), axis=1
    )
    root_ids = jnp.sum(
        jnp.where(jnp.arange(middles_all)[None, :] == middles[:, None], root_of[None, :], 0), axis=1
    )
    path_nodes = jnp.stack(
        [root_ids, roots_all + middles, roots_all + middles_all + request_ids], axis=1
    )
    picked = jnp.arange(nodes_all)[None, None, :] == path_nodes[:, :, None]
    starts = jnp.sum(jnp.where(picked, firsts[None, None, :], 0), axis=2)
    counts = jnp.sum(jnp.where(picked, node_blocks[None, None, :], 0), axis=2)
    ends = jnp.cumsum(counts, axis=1)
    begins = ends - counts
    slots = jnp.arange(3 * MOST_BLK)[None, :]
    which = (slots >= ends[:, 0:1]).astype(jnp.int32) + (slots >= ends[:, 1:2]).astype(jnp.int32)
    which = jnp.minimum(which, 2)
    pick = jnp.arange(3)[None, None, :] == which[:, :, None]
    start_of = jnp.sum(jnp.where(pick, starts[:, None, :], 0), axis=2)
    begin_of = jnp.sum(jnp.where(pick, begins[:, None, :], 0), axis=2)
    ids = start_of + slots - begin_of
    total = ends[:, 2]
    ids = jnp.where(slots < total[:, None], ids, 0)
    return ids.astype(jnp.int32), total.astype(jnp.int32)


def suffix_kernel(q_ref, ks_ref, vs_ref, m_ref, l_ref, acc_ref):
    hd = q_ref.shape[-1]
    contract = (((1,), (1,)), ((), ()))
    scores = lax.dot_general(q_ref[...], ks_ref[...], contract, preferred_element_type=jnp.float32)
    scores = scores * hd ** (-0.5)
    tok = lax.broadcasted_iota(jnp.int32, scores.shape, 0) % SUFFIX
    key = lax.broadcasted_iota(jnp.int32, scores.shape, 1)
    scores = jnp.where(key <= tok, scores, NEG)
    high = jnp.max(scores, axis=-1, keepdims=True)
    weights = jnp.exp(scores - high)
    m_ref[...] = high
    l_ref[...] = jnp.sum(weights, axis=-1, keepdims=True)
    acc_ref[...] = jnp.dot(weights.astype(jnp.bfloat16), vs_ref[...], preferred_element_type=jnp.float32)


def suffix_attend(q, ks, vs):
    req, rows, hd = q.shape
    index = lambda j: (j, 0, 0)
    return pl.pallas_call(
        suffix_kernel,
        out_shape=(
            jax.ShapeDtypeStruct((req, rows, 1), jnp.float32),
            jax.ShapeDtypeStruct((req, rows, 1), jnp.float32),
            jax.ShapeDtypeStruct((req, rows, hd), jnp.float32),
        ),
        grid=(req,),
        in_specs=[
            pl.BlockSpec((None, rows, hd), index),
            pl.BlockSpec((None, SUFFIX, hd), index),
            pl.BlockSpec((None, SUFFIX, hd), index),
        ],
        out_specs=[
            pl.BlockSpec((None, rows, 1), index),
            pl.BlockSpec((None, rows, 1), index),
            pl.BlockSpec((None, rows, hd), index),
        ],
        compiler_params=pltpu.CompilerParams(dimension_semantics=("arbitrary",)),
    )(q, ks, vs)


def attend_kernel(slots, ids_ref, cnt_ref, q_ref, m0_ref, l0_ref, acc0_ref, kv_hbm, o_ref, kbuf, vbuf, sem, m_sc, l_sc, acc_sc):
    j = pl.program_id(0)
    n = cnt_ref[j]
    rows, hd = q_ref.shape
    scale = hd ** (-0.5)
    contract = (((1,), (1,)), ((), ()))
    q = q_ref[...]
    m_sc[...] = m0_ref[...]
    l_sc[...] = l0_ref[...]
    acc_sc[...] = acc0_ref[...]

    rows_blk = kbuf.shape[1] // GROUP
    steps = (n + GROUP - 1) // GROUP

    def copies(step, slot, fresh):
        for g in range(GROUP):
            bid = ids_ref[j * slots + step * GROUP + g] if fresh else 0
            for half, dst in ((0, kbuf), (1, vbuf)):
                yield pltpu.make_async_copy(
                    kv_hbm.at[bid, half],
                    dst.at[slot, pl.ds(g * rows_blk, rows_blk)],
                    sem.at[slot, g, half],
                )

    def fetch(step, slot):
        for c in copies(step, slot, True):
            c.start()

    @pl.when(steps > 0)
    def _():
        fetch(0, 0)

    def body(st, carry):
        slot = st % 2
        for c in copies(st, slot, False):
            c.wait()

        @pl.when(st + 1 < steps)
        def _():
            fetch(st + 1, 1 - slot)

        limit = (n - st * GROUP) * rows_blk

        def update(masked):
            s = lax.dot_general(q, kbuf[slot], contract, preferred_element_type=jnp.float32) * scale
            if masked:
                col = lax.broadcasted_iota(jnp.int32, s.shape, 1)
                s = jnp.where(col < limit, s, NEG)
            m_old = m_sc[...]
            m_new = jnp.maximum(m_old, jnp.max(s, axis=-1, keepdims=True))
            factor = jnp.exp(m_old - m_new)
            p = jnp.exp(s - m_new)
            l_sc[...] = l_sc[...] * factor + jnp.sum(p, axis=-1, keepdims=True)
            acc_sc[...] = acc_sc[...] * factor + jnp.dot(
                p.astype(jnp.bfloat16), vbuf[slot], preferred_element_type=jnp.float32
            )
            m_sc[...] = m_new

        @pl.when(limit >= kbuf.shape[1])
        def _():
            update(False)

        @pl.when(limit < kbuf.shape[1])
        def _():
            update(True)

        return carry

    lax.fori_loop(0, steps, body, 0)
    o_ref[...] = (acc_sc[...] / l_sc[...]).astype(o_ref.dtype)


def attend(ids, counts, q, state, kv_all):
    req, rows, hd = q.shape
    slots = ids.shape[1]
    block_shape = kv_all.shape[1:]
    return pl.pallas_call(
        functools.partial(attend_kernel, slots),
        out_shape=jax.ShapeDtypeStruct((req, rows, hd), jnp.bfloat16),
        grid_spec=pltpu.PrefetchScalarGridSpec(
            num_scalar_prefetch=2,
            grid=(req,),
            in_specs=[
                pl.BlockSpec((None, rows, hd), lambda j, ids, cnt: (j, 0, 0)),
                pl.BlockSpec((None, rows, 1), lambda j, ids, cnt: (j, 0, 0)),
                pl.BlockSpec((None, rows, 1), lambda j, ids, cnt: (j, 0, 0)),
                pl.BlockSpec((None, rows, hd), lambda j, ids, cnt: (j, 0, 0)),
                pl.BlockSpec(memory_space=pl.ANY),
            ],
            out_specs=pl.BlockSpec((None, rows, hd), lambda j, ids, cnt: (j, 0, 0)),
            scratch_shapes=[
                pltpu.VMEM((2, GROUP * block_shape[1], block_shape[2]), kv_all.dtype),
                pltpu.VMEM((2, GROUP * block_shape[1], block_shape[2]), kv_all.dtype),
                pltpu.SemaphoreType.DMA((2, GROUP, 2)),
                pltpu.VMEM((rows, 1), jnp.float32),
                pltpu.VMEM((rows, 1), jnp.float32),
                pltpu.VMEM((rows, hd), jnp.float32),
            ],
        ),
        compiler_params=pltpu.CompilerParams(dimension_semantics=("arbitrary",)),
    )(ids.reshape(-1), counts, q, *state, kv_all)


def exchange_kernel(n, a_ref, w_ref, o_ref, send, recv, send_sem, recv_sem):
    me = lax.axis_index("mem")
    grp = lax.axis_index("grp")
    heads, hd, cols = w_ref.shape
    rows = o_ref.shape[0]
    per_req = a_ref.shape[1] // heads // rows
    barrier = pltpu.get_barrier_semaphore()
    for k in range(1, n):
        pl.semaphore_signal(barrier, inc=1, device_id=(grp, lax.rem(me + k, n)), device_id_type=MESH)
    pl.semaphore_wait(barrier, n - 1)

    def chunk(peer):
        req = peer // per_req
        first = pl.multiple_of((peer % per_req) * rows, rows)
        total = jnp.zeros((rows, cols), jnp.float32)
        for h in range(heads):
            piece = a_ref[req, pl.ds(h * per_req * rows + first, rows), :]
            total = total + jnp.dot(piece, w_ref[h], preferred_element_type=jnp.float32)
        return total.astype(o_ref.dtype)

    n_y = n // 2
    x_hi, y = me // n_y, me % n_y
    shifts = [(a, b) for a in range(2) for b in range(n_y) if (a, b) != (0, 0)]
    shifts.sort(key=lambda ab: -(2 * ab[0] + min(ab[1], n_y - ab[1])))
    copies = []
    for a, b in shifts:
        k = a * n_y + b
        peer = ((x_hi + a) % 2) * n_y + (y + b) % n_y
        send[k] = chunk(peer)
        copy = pltpu.make_async_remote_copy(
            src_ref=send.at[k],
            dst_ref=recv.at[k],
            send_sem=send_sem.at[k],
            recv_sem=recv_sem.at[k],
            device_id=(grp, peer),
            device_id_type=MESH,
        )
        copy.start()
        copies.append((k, copy))
    total = chunk(me).astype(jnp.float32)
    for k, copy in reversed(copies):
        copy.wait()
        total = total + recv[k].astype(jnp.float32)
    o_ref[...] = total.astype(o_ref.dtype)


def exchange_sum(n, attended, w):
    heads, hd, cols = w.shape
    rows = attended.shape[0] * attended.shape[1] // heads // n
    return pl.pallas_call(
        functools.partial(exchange_kernel, n),
        out_shape=jax.ShapeDtypeStruct((rows, cols), jnp.bfloat16),
        in_specs=[pl.BlockSpec(memory_space=pltpu.VMEM)] * 2,
        out_specs=pl.BlockSpec(memory_space=pltpu.VMEM),
        scratch_shapes=[
            pltpu.VMEM((n, rows, cols), jnp.bfloat16),
            pltpu.VMEM((n, rows, cols), jnp.bfloat16),
            pltpu.SemaphoreType.DMA((n,)),
            pltpu.SemaphoreType.DMA((n,)),
        ],
        compiler_params=pltpu.CompilerParams(collective_id=0, has_side_effects=True),
    )(attended, w)


def on_device(n_mem, queries, suffix_kv, prefix_kv, out_weight, node_blocks, root_of, mid_of):
    group_index = lax.axis_index("grp")
    head_index = lax.axis_index("mem")
    tokens_dev, heads_dev, head_dim = queries.shape
    req_local = tokens_dev // SUFFIX
    group_size = QH // KVH
    kv_start = head_index * heads_dev // group_size
    prefix_part = lax.dynamic_index_in_dim(prefix_kv, kv_start, 3, keepdims=False)
    suffix_part = lax.dynamic_index_in_dim(suffix_kv, kv_start, 2, keepdims=False)
    kv_all = lax.all_gather(prefix_part, "grp", axis=0, tiled=True)

    request_ids = group_index * req_local + jnp.arange(req_local)
    ids, counts = path_table(request_ids, node_blocks, root_of, mid_of)

    q = queries.reshape(req_local, SUFFIX, heads_dev, head_dim).transpose(0, 2, 1, 3)
    q = q.reshape(req_local, heads_dev * SUFFIX, head_dim)
    ks = suffix_part[:, 0].reshape(req_local, SUFFIX, head_dim)
    vs = suffix_part[:, 1].reshape(req_local, SUFFIX, head_dim)
    attended = attend(ids, counts, q, suffix_attend(q, ks, vs), kv_all)
    w = out_weight.reshape(heads_dev, head_dim, out_weight.shape[1])
    return exchange_sum(n_mem, attended, w)


def solution(mesh):
    return jax.shard_map(
        functools.partial(on_device, mesh.shape["mem"]),
        mesh=mesh,
        in_specs=(
            P("grp", "mem", None),
            P("grp", None, None, None),
            P("grp", None, None, None, None),
            P("mem", None),
            P(),
            P(),
            P(),
        ),
        out_specs=P(("grp", "mem"), None),
        check_vma=False,
    )
```

```python
import functools

import jax
import jax.numpy as jnp
from jax import lax
from jax.experimental import pallas as pl
from jax.experimental.pallas import tpu as pltpu
from jax.sharding import PartitionSpec as P

QH = 32
KVH = 4
SUFFIX = 256
MOST_BLK = 32
GROUP = 8
NEG = -1e30
MESH = pl.DeviceIdType.MESH


def path_table(request_ids, node_blocks, root_of, mid_of):
    nodes_all = node_blocks.shape[0]
    middles_all = root_of.shape[0]
    leaves = mid_of.shape[0]
    roots_all = nodes_all - middles_all - leaves
    firsts = jnp.cumsum(node_blocks) - node_blocks
    middles = jnp.sum(
        jnp.where(jnp.arange(leaves)[None, :] == request_ids[:, None], mid_of[None, :], 0), axis=1
    )
    root_ids = jnp.sum(
        jnp.where(jnp.arange(middles_all)[None, :] == middles[:, None], root_of[None, :], 0), axis=1
    )
    path_nodes = jnp.stack(
        [root_ids, roots_all + middles, roots_all + middles_all + request_ids], axis=1
    )
    picked = jnp.arange(nodes_all)[None, None, :] == path_nodes[:, :, None]
    starts = jnp.sum(jnp.where(picked, firsts[None, None, :], 0), axis=2)
    counts = jnp.sum(jnp.where(picked, node_blocks[None, None, :], 0), axis=2)
    ends = jnp.cumsum(counts, axis=1)
    begins = ends - counts
    slots = jnp.arange(3 * MOST_BLK)[None, :]
    which = (slots >= ends[:, 0:1]).astype(jnp.int32) + (slots >= ends[:, 1:2]).astype(jnp.int32)
    which = jnp.minimum(which, 2)
    pick = jnp.arange(3)[None, None, :] == which[:, :, None]
    start_of = jnp.sum(jnp.where(pick, starts[:, None, :], 0), axis=2)
    begin_of = jnp.sum(jnp.where(pick, begins[:, None, :], 0), axis=2)
    ids = start_of + slots - begin_of
    total = ends[:, 2]
    ids = jnp.where(slots < total[:, None], ids, 0)
    return ids.astype(jnp.int32), total.astype(jnp.int32)


def suffix_kernel(q_ref, ks_ref, vs_ref, m_ref, l_ref, acc_ref):
    hd = q_ref.shape[-1]
    contract = (((1,), (1,)), ((), ()))
    scores = lax.dot_general(q_ref[...], ks_ref[...], contract, preferred_element_type=jnp.float32)
    scores = scores * hd ** (-0.5)
    tok = lax.broadcasted_iota(jnp.int32, scores.shape, 0) % SUFFIX
    key = lax.broadcasted_iota(jnp.int32, scores.shape, 1)
    scores = jnp.where(key <= tok, scores, NEG)
    high = jnp.max(scores, axis=-1, keepdims=True)
    weights = jnp.exp(scores - high)
    m_ref[...] = high
    l_ref[...] = jnp.sum(weights, axis=-1, keepdims=True)
    acc_ref[...] = jnp.dot(weights.astype(jnp.bfloat16), vs_ref[...], preferred_element_type=jnp.float32)


def suffix_attend(q, ks, vs):
    req, rows, hd = q.shape
    index = lambda j: (j, 0, 0)
    return pl.pallas_call(
        suffix_kernel,
        out_shape=(
            jax.ShapeDtypeStruct((req, rows, 1), jnp.float32),
            jax.ShapeDtypeStruct((req, rows, 1), jnp.float32),
            jax.ShapeDtypeStruct((req, rows, hd), jnp.float32),
        ),
        grid=(req,),
        in_specs=[
            pl.BlockSpec((None, rows, hd), index),
            pl.BlockSpec((None, SUFFIX, hd), index),
            pl.BlockSpec((None, SUFFIX, hd), index),
        ],
        out_specs=[
            pl.BlockSpec((None, rows, 1), index),
            pl.BlockSpec((None, rows, 1), index),
            pl.BlockSpec((None, rows, hd), index),
        ],
        compiler_params=pltpu.CompilerParams(dimension_semantics=("arbitrary",)),
    )(q, ks, vs)


def attend_kernel(slots, ids_ref, cnt_ref, q_ref, m0_ref, l0_ref, acc0_ref, kv_hbm, o_ref, kbuf, vbuf, sem, m_sc, l_sc, acc_sc):
    j = pl.program_id(0)
    n = cnt_ref[j]
    rows, hd = q_ref.shape
    scale = hd ** (-0.5)
    contract = (((1,), (1,)), ((), ()))
    q = q_ref[...]
    m_sc[...] = m0_ref[...]
    l_sc[...] = l0_ref[...]
    acc_sc[...] = acc0_ref[...]

    rows_blk = kbuf.shape[1] // GROUP
    steps = (n + GROUP - 1) // GROUP

    def copies(step, slot, fresh):
        for g in range(GROUP):
            bid = ids_ref[j * slots + step * GROUP + g] if fresh else 0
            for half, dst in ((0, kbuf), (1, vbuf)):
                yield pltpu.make_async_copy(
                    kv_hbm.at[bid, half],
                    dst.at[slot, pl.ds(g * rows_blk, rows_blk)],
                    sem.at[slot, g, half],
                )

    def fetch(step, slot):
        for c in copies(step, slot, True):
            c.start()

    @pl.when(steps > 0)
    def _():
        fetch(0, 0)

    def body(st, carry):
        slot = st % 2
        for c in copies(st, slot, False):
            c.wait()

        @pl.when(st + 1 < steps)
        def _():
            fetch(st + 1, 1 - slot)

        limit = (n - st * GROUP) * rows_blk

        def update(masked):
            s = lax.dot_general(q, kbuf[slot], contract, preferred_element_type=jnp.float32) * scale
            if masked:
                col = lax.broadcasted_iota(jnp.int32, s.shape, 1)
                s = jnp.where(col < limit, s, NEG)
            m_old = m_sc[...]
            m_new = jnp.maximum(m_old, jnp.max(s, axis=-1, keepdims=True))
            factor = jnp.exp(m_old - m_new)
            p = jnp.exp(s - m_new)
            l_sc[...] = l_sc[...] * factor + jnp.sum(p, axis=-1, keepdims=True)
            acc_sc[...] = acc_sc[...] * factor + jnp.dot(
                p.astype(jnp.bfloat16), vbuf[slot], preferred_element_type=jnp.float32
            )
            m_sc[...] = m_new

        @pl.when(limit >= kbuf.shape[1])
        def _():
            update(False)

        @pl.when(limit < kbuf.shape[1])
        def _():
            update(True)

        return carry

    lax.fori_loop(0, steps, body, 0)
    o_ref[...] = (acc_sc[...] / l_sc[...]).astype(o_ref.dtype)


def attend(ids, counts, q, state, kv_all):
    req, rows, hd = q.shape
    slots = ids.shape[1]
    block_shape = kv_all.shape[1:]
    return pl.pallas_call(
        functools.partial(attend_kernel, slots),
        out_shape=jax.ShapeDtypeStruct((req, rows, hd), jnp.bfloat16),
        grid_spec=pltpu.PrefetchScalarGridSpec(
            num_scalar_prefetch=2,
            grid=(req,),
            in_specs=[
                pl.BlockSpec((None, rows, hd), lambda j, ids, cnt: (j, 0, 0)),
                pl.BlockSpec((None, rows, 1), lambda j, ids, cnt: (j, 0, 0)),
                pl.BlockSpec((None, rows, 1), lambda j, ids, cnt: (j, 0, 0)),
                pl.BlockSpec((None, rows, hd), lambda j, ids, cnt: (j, 0, 0)),
                pl.BlockSpec(memory_space=pl.ANY),
            ],
            out_specs=pl.BlockSpec((None, rows, hd), lambda j, ids, cnt: (j, 0, 0)),
            scratch_shapes=[
                pltpu.VMEM((2, GROUP * block_shape[1], block_shape[2]), kv_all.dtype),
                pltpu.VMEM((2, GROUP * block_shape[1], block_shape[2]), kv_all.dtype),
                pltpu.SemaphoreType.DMA((2, GROUP, 2)),
                pltpu.VMEM((rows, 1), jnp.float32),
                pltpu.VMEM((rows, 1), jnp.float32),
                pltpu.VMEM((rows, hd), jnp.float32),
            ],
        ),
        compiler_params=pltpu.CompilerParams(dimension_semantics=("arbitrary",)),
    )(ids.reshape(-1), counts, q, *state, kv_all)


def exchange_kernel(n, a_ref, w_ref, o_ref, send, recv, send_sem, recv_sem):
    me = lax.axis_index("mem")
    grp = lax.axis_index("grp")
    heads, hd, cols = w_ref.shape
    rows = o_ref.shape[0]
    per_req = a_ref.shape[1] // heads // rows
    barrier = pltpu.get_barrier_semaphore()
    for k in range(1, n):
        pl.semaphore_signal(barrier, inc=1, device_id=(grp, lax.rem(me + k, n)), device_id_type=MESH)

    def chunk(peer):
        req = peer // per_req
        first = pl.multiple_of((peer % per_req) * rows, rows)
        total = jnp.zeros((rows, cols), jnp.float32)
        for h in range(heads):
            piece = a_ref[req, pl.ds(h * per_req * rows + first, rows), :]
            total = total + jnp.dot(piece, w_ref[h], preferred_element_type=jnp.float32)
        return total.astype(o_ref.dtype)

    n_y = n // 2
    x_hi, y = me // n_y, me % n_y
    shifts = [(a, b) for a in range(2) for b in range(n_y) if (a, b) != (0, 0)]
    shifts.sort(key=lambda ab: -(2 * ab[0] + min(ab[1], n_y - ab[1])))
    copies = []
    for a, b in shifts:
        k = a * n_y + b
        peer = ((x_hi + a) % 2) * n_y + (y + b) % n_y
        send[k] = chunk(peer)
        if not copies:
            pl.semaphore_wait(barrier, n - 1)
        copy = pltpu.make_async_remote_copy(
            src_ref=send.at[k],
            dst_ref=recv.at[k],
            send_sem=send_sem.at[k],
            recv_sem=recv_sem.at[k],
            device_id=(grp, peer),
            device_id_type=MESH,
        )
        copy.start()
        copies.append((k, copy))
    total = chunk(me).astype(jnp.float32)
    for k, copy in reversed(copies):
        copy.wait()
        total = total + recv[k].astype(jnp.float32)
    o_ref[...] = total.astype(o_ref.dtype)


def exchange_sum(n, attended, w):
    heads, hd, cols = w.shape
    rows = attended.shape[0] * attended.shape[1] // heads // n
    return pl.pallas_call(
        functools.partial(exchange_kernel, n),
        out_shape=jax.ShapeDtypeStruct((rows, cols), jnp.bfloat16),
        in_specs=[pl.BlockSpec(memory_space=pltpu.VMEM)] * 2,
        out_specs=pl.BlockSpec(memory_space=pltpu.VMEM),
        scratch_shapes=[
            pltpu.VMEM((n, rows, cols), jnp.bfloat16),
            pltpu.VMEM((n, rows, cols), jnp.bfloat16),
            pltpu.SemaphoreType.DMA((n,)),
            pltpu.SemaphoreType.DMA((n,)),
        ],
        compiler_params=pltpu.CompilerParams(collective_id=0, has_side_effects=True),
    )(attended, w)


def on_device(n_mem, queries, suffix_kv, prefix_kv, out_weight, node_blocks, root_of, mid_of):
    group_index = lax.axis_index("grp")
    head_index = lax.axis_index("mem")
    tokens_dev, heads_dev, head_dim = queries.shape
    req_local = tokens_dev // SUFFIX
    group_size = QH // KVH
    kv_start = head_index * heads_dev // group_size
    prefix_part = lax.dynamic_index_in_dim(prefix_kv, kv_start, 3, keepdims=False)
    suffix_part = lax.dynamic_index_in_dim(suffix_kv, kv_start, 2, keepdims=False)
    kv_all = lax.all_gather(prefix_part, "grp", axis=0, tiled=True)

    request_ids = group_index * req_local + jnp.arange(req_local)
    ids, counts = path_table(request_ids, node_blocks, root_of, mid_of)

    q = queries.reshape(req_local, SUFFIX, heads_dev, head_dim).transpose(0, 2, 1, 3)
    q = q.reshape(req_local, heads_dev * SUFFIX, head_dim)
    ks = suffix_part[:, 0].reshape(req_local, SUFFIX, head_dim)
    vs = suffix_part[:, 1].reshape(req_local, SUFFIX, head_dim)
    attended = attend(ids, counts, q, suffix_attend(q, ks, vs), kv_all)
    w = out_weight.reshape(heads_dev, head_dim, out_weight.shape[1])
    return exchange_sum(n_mem, attended, w)


def solution(mesh):
    return jax.shard_map(
        functools.partial(on_device, mesh.shape["mem"]),
        mesh=mesh,
        in_specs=(
            P("grp", "mem", None),
            P("grp", None, None, None),
            P("grp", None, None, None, None),
            P("mem", None),
            P(),
            P(),
            P(),
        ),
        out_specs=P(("grp", "mem"), None),
        check_vma=False,
    )
```
